32 devices in a mesh: region: 2 (over x), var: 8 (over z, y), samp: 2 (over core).
Axes of the slice: x: 2, y: 2, z: 4, core: 2. Of those that a mesh axis runs over, the one named last changes fastest.
Arguments:
- dosage: bfloat16 [2048, 16384], P('samp', ('region', 'var')), parts along dimension 1, may hold values from 0 to 2
- observed: int32 [2048, 16384], P('samp', ('region', 'var')), parts along dimension 1, may hold values from 0 to 1, as said below
- counts: int32 [16], P(('region', 'var')), parts along dimension 0, may hold values from 1 to 4, as said below
Outputs:
- correlations: bfloat16 [16, 4, 1024, 1024], P(('region', 'var'), None, 'samp'), parts along dimension 0
The draws below stay inside these ranges and needn't reach their ends.
There are 2 independent parts, one for each index of `region`. The reference program is written for one: setup_inputs(seed, part) draws one part's arguments, and reference() takes and returns one part's arrays. A program takes and returns all parts, laid end to end along the dimension named above; each array names one. Nothing has to cross between parts.
Inputs may be any that keep to these rules, and one draw needn't show every extreme that they name: Block b's partners are blocks b to b + counts[b] - 1; counts[b] is at most 8 - b, and counts[0] = 4. `observed`: some variants are missing in every sample.
All inputs are finite; a program needn't handle non-finite values.
Results may differ from the reference program's by a relative error of at most 0.001.
The reference program's roundings to bfloat16 on the way (of `scored`) count: a program that leaves them out, or rounds other values in their place, can miss the bound.
Values may be sent and summed in bfloat16 or wider, within the bound.
A program may use at most 128 MiB of HBM per device.

```python
import jax
import jax.numpy as jnp
from jax import lax

BLK = 1024
WIN = 4
NBLK = 8
V = 8192
S = 2048


def draw_dosage(key, part):
    spacings = [16, 128, 1024, 4096]
    strengths = [0.25, 0.25, 0.35, 0.45]
    column = jnp.arange(V, dtype=jnp.int32)
    smooth = jnp.zeros((S, V), jnp.float32)
    for number in range(4):
        spacing = spacings[number]
        anchors = jax.random.normal(jax.random.fold_in(key, 11 + number), (S, V // spacing + 2), jnp.float32)
        index = column // spacing
        weight = (column % spacing).astype(jnp.float32) / spacing
        smooth = smooth + strengths[number] * (anchors[:, index] * (1.0 - weight) + anchors[:, index + 1] * weight)
    base = jax.random.uniform(jax.random.fold_in(key, 21), (1, V), jnp.float32, 0.3, 1.7)
    noise = 0.25 * jax.random.normal(jax.random.fold_in(key, 22), (S, V), jnp.float32)
    return jnp.clip(base + smooth + noise, 0.0, 2.0).astype(jnp.bfloat16)


def draw_observed(key, part):
    entries = jax.random.randint(jax.random.fold_in(key, 41), (S, V), 0, 10, dtype=jnp.int32)
    present = (entries < 9).astype(jnp.int32)
    lottery = jax.random.randint(jax.random.fold_in(key, 42), (V,), 0, 64, dtype=jnp.int32)
    forced = jax.random.randint(jax.random.fold_in(key, 43), (), 0, V, dtype=jnp.int32)
    column = jnp.arange(V, dtype=jnp.int32)
    missing = jnp.logical_or(lottery == 0, column == forced)
    return jnp.where(missing[None, :], jnp.zeros_like(present), present)


def draw_counts(key, part):
    drawn = jax.random.randint(jax.random.fold_in(key, 31), (NBLK,), 1, WIN + 1, dtype=jnp.int32)
    limit = NBLK - jnp.arange(NBLK, dtype=jnp.int32)
    capped = jnp.minimum(drawn, limit)
    return capped.at[0].set(WIN)


def setup_inputs(seed: int = 0, part: int = 0) -> dict:
    key_list = jax.random.split(jax.random.key(seed), 4)
    own_keys = jax.random.split(jax.random.fold_in(key_list[3], part), 4)
    return {
        "dosage": draw_dosage(jax.random.fold_in(jax.random.fold_in(key_list[3], part), 71), part),
        "observed": draw_observed(jax.random.fold_in(jax.random.fold_in(key_list[3], part), 71), part),
        "counts": draw_counts(jax.random.fold_in(jax.random.fold_in(key_list[3], part), 71), part),
    }


def reference(dosage, observed, counts):
    values = dosage.astype(jnp.float32)
    present = observed.astype(jnp.float32)
    present_count = jnp.maximum(lax.optimization_barrier(jnp.sum(present, axis=0)), 1.0)
    center = lax.optimization_barrier(jnp.sum(present * values, axis=0)) / present_count
    offsets = present * (values - center)
    spread = lax.optimization_barrier(jnp.sum(offsets * offsets, axis=0)) / present_count
    scored = (offsets * lax.rsqrt(spread + 1e-05)).astype(jnp.bfloat16)

    def one_block(block):
        own = lax.dynamic_slice_in_dim(scored, block * BLK, BLK, 1)
        tiles = []
        for offset in range(WIN):
            target = jnp.minimum(block + offset, NBLK - 1).astype(jnp.int32)
            partner = lax.dynamic_slice_in_dim(scored, target * BLK, BLK, 1)
            product = jnp.dot(own.T, partner, preferred_element_type=jnp.float32) / S
            keep = offset < counts[block]
            tiles.append(jnp.where(keep, product, jnp.zeros_like(product)))
        return jnp.stack(tiles).astype(jnp.bfloat16)
    return lax.map(one_block, jnp.arange(NBLK, dtype=jnp.int32))
```

```python
import functools

import jax
import jax.numpy as jnp
from jax import lax
from jax.experimental import pallas as pl
from jax.experimental.pallas import tpu as pltpu
from jax.sharding import PartitionSpec as P

WIN = 4

epsilon = 1e-05

LANES = 128
WIDTH = 2 * LANES
ROWS = 128
SPLIT = 8
TURNED = 64
BEHIND = 128
STRAIGHT = ((2, 2),)
ROUND = ((0, 1), (1, 1), (4, 1), (5, 1), (6, 1), (7, 1))
VMEM_LIMIT = 40 * 1024 * 1024


def kernel(
    n,
    total,
    d_hbm,
    o_hbm,
    out_ref,
    d_ref,
    o_ref,
    s0,
    s1,
    s2,
    t0,
    tm,
    r2s,
    r3s,
    stat_mine,
    stat_other,
    obuf,
    in_sem,
    stat_sem,
    own_sem,
    down_sem,
    relay_sem,
    y_sem,
    up_sem,
    round_sem,
    x1_sem,
    x2_sem,
    r2_sem,
    r3_sem,
    out_sem,
):
    b = lax.axis_index("var")
    c = lax.axis_index("samp")
    even = lax.rem(b, 2) == 0
    odd = jnp.logical_not(even)
    pair = b + 1 - 2 * lax.rem(b, 2)
    has_up = b + 2 < n
    has_down = b >= 2
    core = {"samp": 1 - c}
    below, above, beside = {"var": b - 2}, {"var": b + 2}, {"var": pair}
    groups, _, full, _ = s0.shape
    local = full // 2
    rows_out = t0.shape[0]
    steps = local // ROWS
    folds = ROWS // 8
    piece = full // SPLIT
    mesh_id = pl.DeviceIdType.MESH
    order = [g for r in range(groups // 2) for g in (r, groups // 2 + r)]
    down_units = [(0, p, k) for p, k in STRAIGHT] + [
        (g, h * (SPLIT // 2), SPLIT // 2) for g in order[1:] for h in range(2)
    ]
    round_units = [(0, p, k) for p, k in ROUND]

    def load(g):
        cols = pl.ds(g * WIDTH, WIDTH)
        return (
            pltpu.make_async_copy(o_hbm.at[:, cols], o_ref.at[g], in_sem.at[g, 0]),
            pltpu.make_async_copy(d_hbm.at[:, cols], d_ref.at[g], in_sem.at[g, 1]),
        )

    for g in order:
        for copy in load(g):
            copy.start()

    def remote(src, dst, sem, where):
        return pltpu.make_async_remote_copy(
            src_ref=src,
            dst_ref=dst,
            send_sem=sem.at[0],
            recv_sem=sem.at[1],
            device_id=where,
            device_id_type=mesh_id,
        )

    barrier = pltpu.get_barrier_semaphore()
    pl.semaphore_signal(barrier, inc=1, device_id=core, device_id_type=mesh_id)
    pl.semaphore_signal(barrier, inc=1, device_id=beside, device_id_type=mesh_id)

    @pl.when(has_up)
    def _():
        pl.semaphore_signal(barrier, inc=1, device_id=above, device_id_type=mesh_id)

    @pl.when(has_down)
    def _():
        pl.semaphore_signal(barrier, inc=1, device_id=below, device_id_type=mesh_id)

    def fold(x):
        return jnp.sum(x.reshape(folds, 8, x.shape[-1]), axis=0)

    def block_rows(r):
        return pl.ds(pl.multiple_of(r * ROWS, ROWS), ROWS)

    def read(g, r, cols):
        present = o_ref[g, block_rows(r), cols].astype(jnp.float32)
        return present, d_ref[g, block_rows(r), cols].astype(jnp.float32)

    stat_mine[...] = jnp.zeros_like(stat_mine)

    def sums(g):
        for copy in load(g):
            copy.wait()
        zero = jnp.zeros((8, WIDTH), jnp.float32)
        everything = slice(0, WIDTH)

        def first(r, carry):
            present, values = read(g, r, everything)
            return carry[0] + fold(present), carry[1] + fold(present * values)

        count8, sum8 = lax.fori_loop(0, steps, first, (zero, zero))
        count = jnp.sum(count8, axis=0, keepdims=True)
        summed = jnp.sum(sum8, axis=0, keepdims=True)
        mean = summed / jnp.maximum(count, 1.0)

        def second(r, carry):
            present, values = read(g, r, everything)
            off = present * (values - mean)
            return carry + fold(off * off)

        square = jnp.sum(lax.fori_loop(0, steps, second, zero), axis=0, keepdims=True)
        stat_mine[g, 0:1, :] = count
        stat_mine[g, 1:2, :] = summed
        stat_mine[g, 2:3, :] = square

    def stat_copy(g):
        return remote(stat_mine.at[g], stat_other.at[g], stat_sem.at[g], core)

    sums(order[0])
    pl.semaphore_wait(barrier, 2 + has_up.astype(jnp.int32) + has_down.astype(jnp.int32))
    stat_copy(order[0]).start()

    def score(g, who):
        cols = pl.ds(pl.multiple_of(who * LANES, LANES), LANES)
        n_a, n_b = stat_mine[g, 0:1, cols], stat_other[g, 0:1, cols]
        s_a, s_b = stat_mine[g, 1:2, cols], stat_other[g, 1:2, cols]
        count = jnp.maximum(n_a + n_b, 1.0)
        center = (s_a + s_b) / count
        gap_a = s_a / jnp.maximum(n_a, 1.0) - center
        gap_b = s_b / jnp.maximum(n_b, 1.0) - center
        square = (stat_mine[g, 2:3, cols] + n_a * gap_a * gap_a) + (
            stat_other[g, 2:3, cols] + n_b * gap_b * gap_b
        )
        scale = lax.rsqrt(square / count + epsilon)

        def third(r, carry):
            present, values = read(g, r, cols)
            out = (present * (values - center) * scale).astype(jnp.bfloat16)
            s0[g, who, pl.ds(pl.multiple_of(c * local + r * ROWS, ROWS), ROWS), :] = out
            return carry

        lax.fori_loop(0, steps, third, 0)

    def part(ref, unit):
        g, first, count = unit
        at = lax.rem(first + c * (SPLIT // 2), SPLIT)
        return ref.at[g, c, pl.ds(pl.multiple_of(at * piece, piece), count * piece), :]

    def samples_of(who, g, stripe):
        return s0.at[g, stripe, pl.ds(pl.multiple_of(who * local, local), local), :]

    def to_core(g, own):
        ref = samples_of(c, g, c if own else 1 - c)
        return remote(ref, ref, own_sem.at[g, 1 if own else 0], core)

    def from_core(g, own):
        ref = samples_of(1 - c, g, c if own else 1 - c)
        return remote(ref, ref, own_sem.at[g, 0 if own else 1], core)

    def down_copy(u):
        unit = down_units[u]
        return remote(part(s0, unit), part(s2, unit), down_sem.at[u], below)

    def down_got(u):
        ref = part(s2, down_units[u])
        return remote(ref, ref, down_sem.at[u], above)

    def relay_copy(u):
        unit = down_units[u]
        return remote(part(s2, unit), part(s1, unit), relay_sem.at[u], beside)

    def relay_got(u):
        ref = part(s1, down_units[u])
        return remote(ref, ref, relay_sem.at[u], beside)

    def half_unit(g, h):
        return (g, h * (SPLIT // 2), SPLIT // 2)

    def y_copy(g, h):
        return remote(part(s0, half_unit(g, h)), part(s1, half_unit(g, h)), y_sem.at[g, h], beside)

    def y_got(g, h):
        ref = part(s1, half_unit(g, h))
        return remote(ref, ref, y_sem.at[g, h], beside)

    def round_copy(leg, u):
        unit = round_units[u]
        src, dst, where = ((s0, s2, beside), (s2, s1, below), (s1, s2, beside))[leg]
        return remote(part(src, unit), part(dst, unit), round_sem.at[leg, u], where)

    def round_got(leg, u):
        ref = part((s2, s1, s2)[leg], round_units[u])
        return remote(ref, ref, round_sem.at[leg, u], above if leg == 1 else beside)

    def send_half(g, h):
        lo, hi = h * (SPLIT // 2), (h + 1) * (SPLIT // 2)

        @pl.when(jnp.logical_and(even, has_down))
        def _():
            for u, unit in enumerate(round_units):
                if unit[0] == g and lo <= unit[1] < hi:
                    round_copy(0, u).start()
            for u, unit in enumerate(down_units):
                if unit[0] == g and lo <= unit[1] < hi:
                    down_copy(u).start()

        @pl.when(odd)
        def _():
            y_copy(g, h).start()

    transit = jnp.logical_and(odd, has_down)

    def pass_down(u):
        round_got(0, u).wait_recv()
        round_copy(1, u).start()

    def up_copy(k):
        rows = pl.ds(k * TURNED, TURNED)
        return remote(t0.at[rows, :], tm.at[rows, :], up_sem.at[k], above)

    def up_got(k):
        ref = tm.at[pl.ds(k * TURNED, TURNED), :]
        return remote(ref, ref, up_sem.at[k], below)

    for i, g in enumerate(order):
        later = order[i + 1] if i + 1 < groups else None
        stat_copy(g).wait()
        score(g, c)
        send_half(g, 0)
        score(g, 1 - c)
        to_core(g, False).start()
        to_core(g, True).start()
        if later is not None:
            sums(later)
            stat_copy(later).start()
        from_core(g, True).wait_recv()
        send_half(g, 1)
        from_core(g, False).wait_recv()
        if i % 2 == 1:
            r = i // 2
            mine = c * (groups // 2) + r
            for st in range(2):
                for q in range(4):
                    rows = slice(q * (full // 4), (q + 1) * (full // 4))
                    at = r * WIDTH + st * LANES
                    t0[at : at + LANES, rows] = s0[mine, st, rows, :].T

            @pl.when(has_up)
            def _():
                for k in range(r * (WIDTH // TURNED), (r + 1) * (WIDTH // TURNED)):
                    up_copy(k).start()

            @pl.when(transit)
            def _():
                for u in (0, 1) if r == 0 else (2, 3):
                    pass_down(u)

    def right(s, g):
        return jnp.concatenate([s[g, 0], s[g, 1]], axis=1)

    def column(g):
        start = g * WIDTH
        return pl.ds(start if isinstance(g, int) else pl.multiple_of(start, WIDTH), WIDTH)

    def product(left, s, g):
        acc = jnp.dot(left, right(s, g), preferred_element_type=jnp.float32)
        return (acc * (1.0 / total)).astype(jnp.bfloat16)

    def tile(k, s, g):
        obuf[k, :, column(g)] = product(t0[...], s, g)

    def tile_range(k, s, lo, hi):
        def one(g, carry):
            tile(k, s, g)
            return carry

        lax.fori_loop(lo, hi, one, 0)

    def store(k):
        return pltpu.make_async_copy(obuf.at[k], out_ref.at[k], out_sem.at[k])

    def core_copy(ref, sem, g, mine):
        part_ref = ref.at[g, c if mine else 1 - c]
        return remote(part_ref, part_ref, sem.at[g], core)

    def core_unit(u):
        ref = part(s2, round_units[u])
        return remote(ref, ref, x2_sem.at[groups + u], core)

    def core_unit_got(u):
        g, first, count = round_units[u]
        at = lax.rem(first + (1 - c) * (SPLIT // 2), SPLIT)
        ref = s2.at[g, 1 - c, pl.ds(pl.multiple_of(at * piece, piece), count * piece), :]
        return remote(ref, ref, x2_sem.at[groups + u], core)

    def core_first(mine):
        g, first, count = down_units[0]
        who = c if mine else 1 - c
        at = lax.rem(first + who * (SPLIT // 2), SPLIT)
        ref = s2.at[g, who, pl.ds(pl.multiple_of(at * piece, piece), count * piece), :]
        return remote(ref, ref, x2_sem.at[g], core)

    def r3_copy(start, size, g):
        rows = pl.ds(start, size)
        return remote(r3s.at[g, rows, :], out_ref.at[WIN - 1, rows, column(g)], r3_sem, below)

    def r3_even(r, g):
        start = pl.multiple_of(r * BEHIND, BEHIND)
        r3s[g, pl.ds(start, BEHIND), :] = product(tm[pl.ds(start, BEHIND), :], s1, g)
        r3_copy(start, BEHIND, g).start()

    def r3_odd(k, g):
        start = pl.multiple_of(k * TURNED, TURNED)
        r3s[g, pl.ds(start, TURNED), :] = product(tm[pl.ds(start, TURNED), :], s1, g)
        r3_copy(start, TURNED, g).start()

    def r2_copy(k):
        rows = pl.ds(k * TURNED, TURNED)
        return remote(r2s.at[rows, :], out_ref.at[WIN - 2, rows, :], r2_sem, below)

    def r2_odd(k):
        rows = pl.ds(k * TURNED, TURNED)

        def one(g, carry):
            r2s[rows, column(g)] = product(tm[rows, :], s0, g)
            return carry

        lax.fori_loop(0, groups, one, 0)
        r2_copy(k).start()

    def over(lo, hi, body):
        def one(r, carry):
            body(r)
            return carry

        lax.fori_loop(lo, hi, one, 0)

    @pl.when(even)
    def _():
        def relay(u):
            @pl.when(has_up)
            def _():
                down_got(u).wait_recv()
                relay_copy(u).start()
                if u == 0:
                    core_first(True).start()
                elif u % 2 == 0:
                    core_copy(s2, x2_sem, down_units[u][0], True).start()

        def arrive(g):
            for h in range(2):
                y_got(g, h).wait_recv()
            core_copy(s1, x1_sem, g, True).start()

        def turned(r):
            @pl.when(has_down)
            def _():
                for k in range(r * BEHIND // TURNED, (r + 1) * BEHIND // TURNED):
                    up_got(k).wait_recv()

        def second(i):
            @pl.when(has_up)
            def _():
                g = order[i]
                core_copy(s2, x2_sem, g, False).wait_recv()
                tile(2, s2, g)

        relay(0)
        tile_range(0, s0, 0, groups)
        store(0).start()
        u = 1
        for i in range(groups):
            g = order[i]
            if u < len(down_units):
                relay(u)
                u += 1
            arrive(g)
            if u < len(down_units):
                relay(u)
                u += 1
            core_copy(s1, x1_sem, g, False).wait_recv()

            @pl.when(has_down)
            def _():
                over(0, i, lambda r: r3_even(r, g))

            turned(i)

            @pl.when(has_down)
            def _():
                for j in range(i + 1):
                    r3_even(i, order[j])

            tile(1, s1, g)
            if i >= 1:
                second(i)
        store(1).start()

        @pl.when(has_up)
        def _():
            core_first(False).wait_recv()
            for v in range(len(round_units)):
                round_got(2, v).wait_recv()
                core_unit(v).start()
            for v in range(len(round_units)):
                core_unit_got(v).wait_recv()
            tile(2, s2, 0)

        store(2).start()

        @pl.when(has_up)
        def _():
            pltpu.make_async_remote_copy(
                src_ref=out_ref.at[WIN - 1],
                dst_ref=out_ref.at[WIN - 1],
                send_sem=r3_sem.at[0],
                recv_sem=r3_sem.at[1],
                device_id=above,
                device_id_type=mesh_id,
            ).wait_recv()

        store(2).wait()

    @pl.when(odd)
    def _():
        def turn(k, columns):
            @pl.when(has_down)
            def _():
                up_got(k).wait_recv()
                r2_odd(k)

            @pl.when(jnp.logical_and(has_down, has_up))
            def _():
                for g in columns:
                    r3_odd(k, g)

        def arrive(i, rows):
            g = order[i]

            @pl.when(has_up)
            def _():
                if i == 0:
                    for v in range(len(round_units)):
                        round_got(1, v).wait_recv()
                        round_copy(2, v).start()
                    relay_got(0).wait_recv()
                else:
                    for h in range(2):
                        relay_got(2 * i - 1 + h).wait_recv()
                core_copy(s1, x1_sem, g, True).start()
                core_copy(s1, x1_sem, g, False).wait_recv()

            @pl.when(jnp.logical_and(has_down, has_up))
            def _():
                over(0, rows, lambda k: r3_odd(k, g))

            @pl.when(has_up)
            def _():
                tile(1, s1, g)

        tile_range(0, s0, 0, groups // 2)

        @pl.when(has_down)
        def _():
            pass_down(4)

        tile_range(0, s0, groups // 2, groups)
        store(0).start()

        @pl.when(has_down)
        def _():
            pass_down(5)

        turn(0, [])
        turn(1, [])
        arrive(0, 2)
        turn(2, order[:1])
        arrive(1, 3)
        turn(3, order[:2])
        turn(4, order[:2])
        arrive(2, 5)
        turn(5, order[:3])
        turn(6, order[:3])
        arrive(3, 7)
        turn(7, order)
        store(1).start()

        @pl.when(has_up)
        def _():
            pltpu.make_async_remote_copy(
                src_ref=out_ref.at[WIN - 2],
                dst_ref=out_ref.at[WIN - 2],
                send_sem=r2_sem.at[0],
                recv_sem=r2_sem.at[1],
                device_id=above,
                device_id_type=mesh_id,
            ).wait_recv()

        @pl.when(b + 4 < n)
        def _():
            pltpu.make_async_remote_copy(
                src_ref=out_ref.at[WIN - 1],
                dst_ref=out_ref.at[WIN - 1],
                send_sem=r3_sem.at[0],
                recv_sem=r3_sem.at[1],
                device_id=above,
                device_id_type=mesh_id,
            ).wait_recv()

    for g in range(groups):
        to_core(g, False).wait_send()
        to_core(g, True).wait_send()

    @pl.when(has_up)
    def _():
        for k in range(rows_out // TURNED):
            up_copy(k).wait_send()

    @pl.when(jnp.logical_or(even, has_up))
    def _():
        for g in range(groups):
            core_copy(s1, x1_sem, g, True).wait_send()

    def sent_results(buffer, sem):
        pltpu.make_async_remote_copy(
            src_ref=buffer,
            dst_ref=buffer,
            send_sem=sem.at[0],
            recv_sem=sem.at[1],
            device_id=below,
            device_id_type=mesh_id,
        ).wait_send()

    @pl.when(even)
    def _():
        @pl.when(has_down)
        def _():
            for u in range(len(down_units)):
                down_copy(u).wait_send()
            for u in range(len(round_units)):
                round_copy(0, u).wait_send()
            sent_results(r3s, r3_sem)

        @pl.when(has_up)
        def _():
            for u in range(len(down_units)):
                relay_copy(u).wait_send()
            core_first(True).wait_send()
            for g in order[1:]:
                core_copy(s2, x2_sem, g, True).wait_send()
            for u in range(len(round_units)):
                core_unit(u).wait_send()

    @pl.when(odd)
    def _():
        for g in range(groups):
            for h in range(2):
                y_copy(g, h).wait_send()

        @pl.when(has_down)
        def _():
            for u in range(len(round_units)):
                round_copy(1, u).wait_send()
            sent_results(r2s, r2_sem)

        @pl.when(has_up)
        def _():
            for u in range(len(round_units)):
                round_copy(2, u).wait_send()

        @pl.when(jnp.logical_and(has_down, has_up))
        def _():
            sent_results(r3s, r3_sem)

    store(0).wait()
    store(1).wait()


def per_device(dosage, observed, counts):
    local, variants = dosage.shape
    n = lax.axis_size("var")
    full = local * lax.axis_size("samp")
    half = variants // 2
    groups = variants // WIDTH
    downs = len(STRAIGHT) + 2 * (groups - 1)
    rounds = len(ROUND)
    dma = pltpu.SemaphoreType.DMA
    block = pltpu.VMEM((groups, 2, full, LANES), jnp.bfloat16)
    tiles = pl.pallas_call(
        functools.partial(kernel, n, float(full)),
        out_shape=jax.ShapeDtypeStruct((WIN, half, variants), jnp.bfloat16),
        in_specs=[pl.BlockSpec(memory_space=pltpu.HBM)] * 2,
        out_specs=pl.BlockSpec(memory_space=pl.ANY),
        scratch_shapes=[
            pltpu.VMEM((groups, local, WIDTH), dosage.dtype),
            pltpu.VMEM((groups, local, WIDTH), observed.dtype),
            block,
            block,
            block,
            pltpu.VMEM((half, full), jnp.bfloat16),
            pltpu.VMEM((half, full), jnp.bfloat16),
            pltpu.VMEM((half, variants), jnp.bfloat16),
            pltpu.VMEM((groups, half, WIDTH), jnp.bfloat16),
            pltpu.VMEM((groups, 8, WIDTH), jnp.float32),
            pltpu.VMEM((groups, 8, WIDTH), jnp.float32),
            pltpu.VMEM((WIN - 1, half, variants), jnp.bfloat16),
            dma((groups, 2)),
            dma((groups, 2)),
            dma((groups, 2, 2)),
            dma((downs, 2)),
            dma((downs, 2)),
            dma((groups, 2, 2)),
            dma((half // TURNED, 2)),
            dma((3, rounds, 2)),
            dma((groups, 2)),
            dma((groups + rounds, 2)),
            dma((2,)),
            dma((2,)),
            dma((WIN - 1,)),
        ],
        compiler_params=pltpu.CompilerParams(
            collective_id=0, has_side_effects=True, vmem_limit_bytes=VMEM_LIMIT
        ),
    )(
        pltpu.with_memory_space_constraint(dosage, pltpu.HBM),
        pltpu.with_memory_space_constraint(observed, pltpu.HBM),
    )
    keep = jnp.arange(WIN, dtype=jnp.int32)[:, None, None] < counts[0]
    return jnp.where(keep, tiles, jnp.zeros_like(tiles))[None]


def solution(mesh):
    in_specs = (P("samp", ("region", "var")), P("samp", ("region", "var")), P(("region", "var")))
    out_specs = P(("region", "var"), None, "samp", None)
    return jax.shard_map(
        per_device, mesh=mesh, in_specs=in_specs, out_specs=out_specs, check_vma=False
    )
```

```python
import functools

import jax
import jax.numpy as jnp
from jax import lax
from jax.experimental import pallas as pl
from jax.experimental.pallas import tpu as pltpu
from jax.sharding import PartitionSpec as P

WIN = 4

epsilon = 1e-05

LANES = 128
WIDTH = 2 * LANES
ROWS = 128
SPLIT = 8
TURNED = 64
BEHIND = 128
STRAIGHT = ((2, 2),)
ROUND = ((0, 1), (1, 1), (4, 1), (5, 1), (6, 1), (7, 1))
VMEM_LIMIT = 40 * 1024 * 1024


def kernel(
    n,
    total,
    d_hbm,
    o_hbm,
    out_ref,
    d_ref,
    o_ref,
    s0,
    s1,
    s2,
    t0,
    tu,
    tm,
    r2s,
    r3s,
    stat_mine,
    stat_other,
    obuf,
    in_sem,
    stat_sem,
    own_sem,
    down_sem,
    relay_sem,
    y_sem,
    up_sem,
    round_sem,
    x1_sem,
    x2_sem,
    r2_sem,
    r3_sem,
    out_sem,
):
    b = lax.axis_index("var")
    c = lax.axis_index("samp")
    even = lax.rem(b, 2) == 0
    odd = jnp.logical_not(even)
    pair = b + 1 - 2 * lax.rem(b, 2)
    has_up = b + 2 < n
    has_down = b >= 2
    core = {"samp": 1 - c}
    below, above, beside = {"var": b - 2}, {"var": b + 2}, {"var": pair}
    groups, _, full, _ = s0.shape
    local = full // 2
    rows_out = t0.shape[0]
    steps = local // ROWS
    folds = ROWS // 8
    piece = full // SPLIT
    mesh_id = pl.DeviceIdType.MESH
    order = [g for r in range(groups // 2) for g in (r, groups // 2 + r)]
    down_units = [(0, p, k) for p, k in STRAIGHT] + [
        (g, h * (SPLIT // 2), SPLIT // 2) for g in order[1:] for h in range(2)
    ]
    round_units = [(0, p, k) for p, k in ROUND]

    def load(g):
        cols = pl.ds(g * WIDTH, WIDTH)
        return (
            pltpu.make_async_copy(o_hbm.at[:, cols], o_ref.at[g], in_sem.at[g, 0]),
            pltpu.make_async_copy(d_hbm.at[:, cols], d_ref.at[g], in_sem.at[g, 1]),
        )

    for g in order:
        for copy in load(g):
            copy.start()

    def remote(src, dst, sem, where):
        return pltpu.make_async_remote_copy(
            src_ref=src,
            dst_ref=dst,
            send_sem=sem.at[0],
            recv_sem=sem.at[1],
            device_id=where,
            device_id_type=mesh_id,
        )

    barrier = pltpu.get_barrier_semaphore()
    pl.semaphore_signal(barrier, inc=1, device_id=core, device_id_type=mesh_id)
    pl.semaphore_signal(barrier, inc=1, device_id=beside, device_id_type=mesh_id)

    @pl.when(has_up)
    def _():
        for m in range(2):
            both = {"var": b + 2, "samp": m}
            pl.semaphore_signal(barrier, inc=1, device_id=both, device_id_type=mesh_id)

    @pl.when(has_down)
    def _():
        for m in range(2):
            both = {"var": b - 2, "samp": m}
            pl.semaphore_signal(barrier, inc=1, device_id=both, device_id_type=mesh_id)

    def fold(x):
        return jnp.sum(x.reshape(folds, 8, x.shape[-1]), axis=0)

    def block_rows(r):
        return pl.ds(pl.multiple_of(r * ROWS, ROWS), ROWS)

    def read(g, r, cols):
        present = o_ref[g, block_rows(r), cols].astype(jnp.float32)
        return present, d_ref[g, block_rows(r), cols].astype(jnp.float32)

    stat_mine[...] = jnp.zeros_like(stat_mine)

    def sums(g):
        for copy in load(g):
            copy.wait()
        zero = jnp.zeros((8, WIDTH), jnp.float32)
        everything = slice(0, WIDTH)

        def first(r, carry):
            present, values = read(g, r, everything)
            return carry[0] + fold(present), carry[1] + fold(present * values)

        count8, sum8 = lax.fori_loop(0, steps, first, (zero, zero))
        count = jnp.sum(count8, axis=0, keepdims=True)
        summed = jnp.sum(sum8, axis=0, keepdims=True)
        mean = summed / jnp.maximum(count, 1.0)

        def second(r, carry):
            present, values = read(g, r, everything)
            off = present * (values - mean)
            return carry + fold(off * off)

        square = jnp.sum(lax.fori_loop(0, steps, second, zero), axis=0, keepdims=True)
        stat_mine[g, 0:1, :] = count
        stat_mine[g, 1:2, :] = summed
        stat_mine[g, 2:3, :] = square

    def stat_copy(g):
        return remote(stat_mine.at[g], stat_other.at[g], stat_sem.at[g], core)

    def score(g, who):
        cols = pl.ds(pl.multiple_of(who * LANES, LANES), LANES)
        n_a, n_b = stat_mine[g, 0:1, cols], stat_other[g, 0:1, cols]
        s_a, s_b = stat_mine[g, 1:2, cols], stat_other[g, 1:2, cols]
        count = jnp.maximum(n_a + n_b, 1.0)
        center = (s_a + s_b) / count
        gap_a = s_a / jnp.maximum(n_a, 1.0) - center
        gap_b = s_b / jnp.maximum(n_b, 1.0) - center
        square = (stat_mine[g, 2:3, cols] + n_a * gap_a * gap_a) + (
            stat_other[g, 2:3, cols] + n_b * gap_b * gap_b
        )
        scale = lax.rsqrt(square / count + epsilon)

        def third(r, carry):
            present, values = read(g, r, cols)
            out = (present * (values - center) * scale).astype(jnp.bfloat16)
            s0[g, who, pl.ds(pl.multiple_of(c * local + r * ROWS, ROWS), ROWS), :] = out
            return carry

        lax.fori_loop(0, steps, third, 0)

    def part(ref, unit):
        g, first, count = unit
        at = lax.rem(first + c * (SPLIT // 2), SPLIT)
        return ref.at[g, c, pl.ds(pl.multiple_of(at * piece, piece), count * piece), :]

    def samples_of(who, g, stripe):
        return s0.at[g, stripe, pl.ds(pl.multiple_of(who * local, local), local), :]

    def to_core(g, own):
        ref = samples_of(c, g, c if own else 1 - c)
        return remote(ref, ref, own_sem.at[g, 1 if own else 0], core)

    def from_core(g, own):
        ref = samples_of(1 - c, g, c if own else 1 - c)
        return remote(ref, ref, own_sem.at[g, 0 if own else 1], core)

    def down_copy(u):
        unit = down_units[u]
        return remote(part(s0, unit), part(s2, unit), down_sem.at[u], below)

    def down_got(u):
        ref = part(s2, down_units[u])
        return remote(ref, ref, down_sem.at[u], above)

    def relay_copy(u):
        unit = down_units[u]
        return remote(part(s2, unit), part(s1, unit), relay_sem.at[u], beside)

    def relay_got(u):
        ref = part(s1, down_units[u])
        return remote(ref, ref, relay_sem.at[u], beside)

    def half_unit(g, h):
        return (g, h * (SPLIT // 2), SPLIT // 2)

    def y_copy(g, h):
        return remote(part(s0, half_unit(g, h)), part(s1, half_unit(g, h)), y_sem.at[g, h], beside)

    def y_got(g, h):
        ref = part(s1, half_unit(g, h))
        return remote(ref, ref, y_sem.at[g, h], beside)

    def round_copy(leg, u):
        unit = round_units[u]
        src, dst, where = ((s0, s2, beside), (s2, s1, below), (s1, s2, beside))[leg]
        return remote(part(src, unit), part(dst, unit), round_sem.at[leg, u], where)

    def round_got(leg, u):
        ref = part((s2, s1, s2)[leg], round_units[u])
        return remote(ref, ref, round_sem.at[leg, u], above if leg == 1 else beside)

    def send_half(g, h):
        lo, hi = h * (SPLIT // 2), (h + 1) * (SPLIT // 2)

        @pl.when(jnp.logical_and(even, has_down))
        def _():
            for u, unit in enumerate(round_units):
                if unit[0] == g and lo <= unit[1] < hi:
                    round_copy(0, u).start()
            for u, unit in enumerate(down_units):
                if unit[0] == g and lo <= unit[1] < hi:
                    down_copy(u).start()

        @pl.when(odd)
        def _():
            y_copy(g, h).start()

    transit = jnp.logical_and(odd, has_down)

    def pass_down(u):
        round_got(0, u).wait_recv()
        round_copy(1, u).start()

    def up_copy(k):
        rows = pl.ds(k * TURNED, TURNED)
        return remote(tu.at[rows, :], tm.at[rows, :], up_sem.at[k], above)

    def up_got(k):
        ref = tm.at[pl.ds(k * TURNED, TURNED), :]
        return remote(ref, ref, up_sem.at[k], below)

    def finish(g):
        score(g, c)
        send_half(g, 0)
        score(g, 1 - c)
        to_core(g, False).start()
        to_core(g, True).start()

    def complete(i):
        g = order[i]
        from_core(g, True).wait_recv()
        send_half(g, 1)

        @pl.when(has_up)
        def _():
            for q in range(4):
                rows = slice(q * (full // 4), (q + 1) * (full // 4))
                tu[i * LANES : (i + 1) * LANES, rows] = s0[g, c, rows, :].T
            for k in range(i * (LANES // TURNED), (i + 1) * (LANES // TURNED)):
                up_copy(k).start()

    def turn_own():
        def one(r, carry):
            for st in range(2):
                for q in range(4):
                    rows = slice(q * (full // 4), (q + 1) * (full // 4))
                    at = pl.multiple_of(r * WIDTH + st * LANES, LANES)
                    t0[pl.ds(at, LANES), rows] = s0[c * (groups // 2) + r, st, rows, :].T
            return carry

        lax.fori_loop(0, groups // 2, one, 0)

    def pass_some(units):
        @pl.when(transit)
        def _():
            for u in units:
                pass_down(u)

    sums(order[0])
    pl.semaphore_wait(barrier, 2 + 2 * (has_up.astype(jnp.int32) + has_down.astype(jnp.int32)))
    stat_copy(order[0]).start()
    for i, g in enumerate(order):
        if i + 1 < groups:
            sums(order[i + 1])
            stat_copy(order[i + 1]).start()
        if i > 0:
            complete(i - 1)
        if i >= 2:
            pass_some((i - 1,))
        stat_copy(g).wait()
        finish(g)
        if i == 1:
            pass_some((0,))
    pass_some((3,))
    complete(groups - 1)
    pass_some((4,))
    for g in order:
        from_core(g, False).wait_recv()
    turn_own()

    def right(s, g):
        return jnp.concatenate([s[g, 0], s[g, 1]], axis=1)

    def column(g):
        start = g * WIDTH
        return pl.ds(start if isinstance(g, int) else pl.multiple_of(start, WIDTH), WIDTH)

    def product(left, s, g):
        acc = jnp.dot(left, right(s, g), preferred_element_type=jnp.float32)
        return (acc * (1.0 / total)).astype(jnp.bfloat16)

    def tile(k, s, g):
        obuf[k, :, column(g)] = product(t0[...], s, g)

    def tile_range(k, s, lo, hi):
        def one(g, carry):
            tile(k, s, g)
            return carry

        lax.fori_loop(lo, hi, one, 0)

    def store(k):
        return pltpu.make_async_copy(obuf.at[k], out_ref.at[k], out_sem.at[k])

    def core_copy(ref, sem, g, mine):
        part_ref = ref.at[g, c if mine else 1 - c]
        return remote(part_ref, part_ref, sem.at[g], core)

    def core_unit(u):
        ref = part(s2, round_units[u])
        return remote(ref, ref, x2_sem.at[groups + u], core)

    def core_unit_got(u):
        g, first, count = round_units[u]
        at = lax.rem(first + (1 - c) * (SPLIT // 2), SPLIT)
        ref = s2.at[g, 1 - c, pl.ds(pl.multiple_of(at * piece, piece), count * piece), :]
        return remote(ref, ref, x2_sem.at[groups + u], core)

    def core_first(mine):
        g, first, count = down_units[0]
        who = c if mine else 1 - c
        at = lax.rem(first + who * (SPLIT // 2), SPLIT)
        ref = s2.at[g, who, pl.ds(pl.multiple_of(at * piece, piece), count * piece), :]
        return remote(ref, ref, x2_sem.at[g], core)

    def behind_to(start, size, k, cols):
        i = start // LANES
        at = (i // 2) * WIDTH + c * LANES + lax.rem(start, LANES)
        rows = pl.ds(pl.multiple_of(at, TURNED), size)
        return out_ref.at[k, rows, cols], {"var": b - 2, "samp": lax.rem(i, 2)}

    def r3_send(start, size, g):
        rows = pl.ds(start, size)
        r3s[g, rows, :] = product(tm[rows, :], s1, g)
        dst, where = behind_to(start, size, WIN - 1, column(g))
        remote(r3s.at[g, rows, :], dst, r3_sem, where).start()

    def r3_even(r, g):
        r3_send(pl.multiple_of(r * BEHIND, BEHIND), BEHIND, g)

    def r3_odd(k, g):
        r3_send(pl.multiple_of(k * TURNED, TURNED), TURNED, g)

    def r2_odd(k):
        rows = pl.ds(k * TURNED, TURNED)

        def one(g, carry):
            r2s[rows, column(g)] = product(tm[rows, :], s0, g)
            return carry

        lax.fori_loop(0, groups, one, 0)
        dst, where = behind_to(jnp.int32(k * TURNED), TURNED, WIN - 2, slice(None))
        remote(r2s.at[rows, :], dst, r2_sem, where).start()

    def over(lo, hi, body):
        def one(r, carry):
            body(r)
            return carry

        lax.fori_loop(lo, hi, one, 0)

    def drain_common():
        for g in range(groups):
            to_core(g, False).wait_send()
            to_core(g, True).wait_send()

        @pl.when(has_up)
        def _():
            for k in range(rows_out // TURNED):
                up_copy(k).wait_send()

        @pl.when(jnp.logical_or(even, has_up))
        def _():
            for g in range(groups):
                core_copy(s1, x1_sem, g, True).wait_send()

    def sent_results(buffer, sem):
        remote(buffer, buffer, sem, below).wait_send()

    def got_results(k, sem):
        remote(out_ref.at[k], out_ref.at[k], sem, above).wait_recv()

    @pl.when(even)
    def _():
        def relay(u):
            @pl.when(has_up)
            def _():
                down_got(u).wait_recv()
                relay_copy(u).start()
                if u == 0:
                    core_first(True).start()
                elif u % 2 == 0:
                    core_copy(s2, x2_sem, down_units[u][0], True).start()

        def arrive(g):
            for h in range(2):
                y_got(g, h).wait_recv()
            core_copy(s1, x1_sem, g, True).start()

        def turned(r):
            @pl.when(has_down)
            def _():
                for k in range(r * BEHIND // TURNED, (r + 1) * BEHIND // TURNED):
                    up_got(k).wait_recv()

        def second(i):
            @pl.when(has_up)
            def _():
                g = order[i]
                core_copy(s2, x2_sem, g, False).wait_recv()
                tile(2, s2, g)

        relay(0)
        tile_range(0, s0, 0, groups)
        store(0).start()
        u = 1
        for i in range(groups):
            g = order[i]
            if u < len(down_units):
                relay(u)
                u += 1
            arrive(g)
            if u < len(down_units):
                relay(u)
                u += 1
            core_copy(s1, x1_sem, g, False).wait_recv()

            @pl.when(has_down)
            def _():
                over(0, i, lambda r: r3_even(r, g))

            turned(i)

            @pl.when(has_down)
            def _():
                for j in range(i + 1):
                    r3_even(i, order[j])

            tile(1, s1, g)
            if i >= 1:
                second(i)
        store(1).start()
        drain_common()

        @pl.when(has_down)
        def _():
            for v in range(len(down_units)):
                down_copy(v).wait_send()
            for v in range(len(round_units)):
                round_copy(0, v).wait_send()

        @pl.when(has_up)
        def _():
            for v in range(len(down_units)):
                relay_copy(v).wait_send()
            core_first(True).wait_send()
            for g in order[1:]:
                core_copy(s2, x2_sem, g, True).wait_send()
            core_first(False).wait_recv()
            for v in range(len(round_units)):
                round_got(2, v).wait_recv()
                core_unit(v).start()
            for v in range(len(round_units)):
                core_unit_got(v).wait_recv()
            tile(2, s2, 0)
            store(2).start()
            for v in range(len(round_units)):
                core_unit(v).wait_send()

        @pl.when(has_down)
        def _():
            sent_results(r3s, r3_sem)

        @pl.when(has_up)
        def _():
            got_results(WIN - 1, r3_sem)
            store(2).wait()

    @pl.when(odd)
    def _():
        def turn(k, columns):
            @pl.when(has_down)
            def _():
                up_got(k).wait_recv()
                r2_odd(k)

            @pl.when(jnp.logical_and(has_down, has_up))
            def _():
                for g in columns:
                    r3_odd(k, g)

        def arrive(i, rows):
            g = order[i]

            @pl.when(has_up)
            def _():
                if i == 0:
                    for v in range(len(round_units)):
                        round_got(1, v).wait_recv()
                        round_copy(2, v).start()
                    relay_got(0).wait_recv()
                else:
                    for h in range(2):
                        relay_got(2 * i - 1 + h).wait_recv()
                core_copy(s1, x1_sem, g, True).start()
                core_copy(s1, x1_sem, g, False).wait_recv()

            @pl.when(jnp.logical_and(has_down, has_up))
            def _():
                over(0, rows, lambda k: r3_odd(k, g))

        def first(i):
            @pl.when(has_up)
            def _():
                tile(1, s1, order[i])

        @pl.when(has_down)
        def _():
            pass_down(5)

        turn(0, [])
        tile_range(0, s0, 0, groups)
        store(0).start()
        turn(1, [])
        arrive(0, 2)
        turn(2, order[:1])
        first(0)
        arrive(1, 3)
        turn(3, order[:2])
        first(1)
        turn(4, order[:2])
        arrive(2, 5)
        turn(5, order[:3])
        first(2)
        turn(6, order[:3])
        arrive(3, 7)
        turn(7, order)
        first(3)
        store(1).start()
        drain_common()
        for g in range(groups):
            for h in range(2):
                y_copy(g, h).wait_send()

        @pl.when(has_down)
        def _():
            for v in range(len(round_units)):
                round_copy(1, v).wait_send()

        @pl.when(has_up)
        def _():
            for v in range(len(round_units)):
                round_copy(2, v).wait_send()

        @pl.when(has_down)
        def _():
            sent_results(r2s, r2_sem)

        @pl.when(jnp.logical_and(has_down, has_up))
        def _():
            sent_results(r3s, r3_sem)

        @pl.when(has_up)
        def _():
            got_results(WIN - 2, r2_sem)

        @pl.when(b + 4 < n)
        def _():
            got_results(WIN - 1, r3_sem)

    store(0).wait()
    store(1).wait()


def per_device(dosage, observed, counts):
    local, variants = dosage.shape
    n = lax.axis_size("var")
    full = local * lax.axis_size("samp")
    half = variants // 2
    groups = variants // WIDTH
    downs = len(STRAIGHT) + 2 * (groups - 1)
    rounds = len(ROUND)
    dma = pltpu.SemaphoreType.DMA
    block = pltpu.VMEM((groups, 2, full, LANES), jnp.bfloat16)
    tiles = pl.pallas_call(
        functools.partial(kernel, n, float(full)),
        out_shape=jax.ShapeDtypeStruct((WIN, half, variants), jnp.bfloat16),
        in_specs=[pl.BlockSpec(memory_space=pltpu.HBM)] * 2,
        out_specs=pl.BlockSpec(memory_space=pl.ANY),
        scratch_shapes=[
            pltpu.VMEM((groups, local, WIDTH), dosage.dtype),
            pltpu.VMEM((groups, local, WIDTH), observed.dtype),
            block,
            block,
            block,
            pltpu.VMEM((half, full), jnp.bfloat16),
            pltpu.VMEM((half, full), jnp.bfloat16),
            pltpu.VMEM((half, full), jnp.bfloat16),
            pltpu.VMEM((half, variants), jnp.bfloat16),
            pltpu.VMEM((groups, half, WIDTH), jnp.bfloat16),
            pltpu.VMEM((groups, 8, WIDTH), jnp.float32),
            pltpu.VMEM((groups, 8, WIDTH), jnp.float32),
            pltpu.VMEM((WIN - 1, half, variants), jnp.bfloat16),
            dma((groups, 2)),
            dma((groups, 2)),
            dma((groups, 2, 2)),
            dma((downs, 2)),
            dma((downs, 2)),
            dma((groups, 2, 2)),
            dma((half // TURNED, 2)),
            dma((3, rounds, 2)),
            dma((groups, 2)),
            dma((groups + rounds, 2)),
            dma((2,)),
            dma((2,)),
            dma((WIN - 1,)),
        ],
        compiler_params=pltpu.CompilerParams(
            collective_id=0, has_side_effects=True, vmem_limit_bytes=VMEM_LIMIT
        ),
    )(
        pltpu.with_memory_space_constraint(dosage, pltpu.HBM),
        pltpu.with_memory_space_constraint(observed, pltpu.HBM),
    )
    keep = jnp.arange(WIN, dtype=jnp.int32)[:, None, None] < counts[0]
    return jnp.where(keep, tiles, jnp.zeros_like(tiles))[None]


def solution(mesh):
    in_specs = (P("samp", ("region", "var")), P("samp", ("region", "var")), P(("region", "var")))
    out_specs = P(("region", "var"), None, "samp", None)
    return jax.shard_map(
        per_device, mesh=mesh, in_specs=in_specs, out_specs=out_specs, check_vma=False
    )
```

```python
import functools

import jax
import jax.numpy as jnp
from jax import lax
from jax.experimental import pallas as pl
from jax.experimental.pallas import tpu as pltpu
from jax.sharding import PartitionSpec as P

WIN = 4

epsilon = 1e-05

LANES = 128
WIDTH = 2 * LANES
ROWS = 128
SPLIT = 4
TURNED = 64
STRAIGHT = ((1, 3, 1),)
ROUND = ((0, 0, 1), (0, 1, 1), (0, 2, 1), (0, 3, 1), (1, 0, 1), (1, 1, 1), (1, 2, 1))
VMEM_LIMIT = 40 * 1024 * 1024


def kernel(
    n,
    total,
    d_hbm,
    o_hbm,
    out_ref,
    d_ref,
    o_ref,
    s0,
    s1,
    s2,
    t0,
    tu,
    tm,
    r2s,
    r3s,
    stat_mine,
    stat_other,
    obuf,
    in_sem,
    stat_sem,
    own_sem,
    down_sem,
    relay_sem,
    y_sem,
    up_sem,
    round_sem,
    x1_sem,
    x2_sem,
    r2_sem,
    r3_sem,
    ahead_sem,
    out_sem,
):
    b = lax.axis_index("var")
    c = lax.axis_index("samp")
    even = lax.rem(b, 2) == 0
    odd = jnp.logical_not(even)
    pair = b + 1 - 2 * lax.rem(b, 2)
    has_up = b + 2 < n
    has_down = b >= 2
    core = {"samp": 1 - c}
    below, above, beside = {"var": b - 2}, {"var": b + 2}, {"var": pair}
    groups, _, full, _ = s0.shape
    local = full // 2
    rows_out = t0.shape[0]
    steps = local // ROWS
    folds = ROWS // 8
    piece = local // SPLIT
    mesh_id = pl.DeviceIdType.MESH
    order = [g for r in range(groups // 2) for g in (r, groups // 2 + r)]
    stripes = [(g, st) for g in order for st in range(2)]
    down_units = [(0, st, p, k) for st, p, k in STRAIGHT] + [(g, st, 0, SPLIT) for g, st in stripes[2:]]
    round_units = [(0, st, p, k) for st, p, k in ROUND]

    def load(g):
        cols = pl.ds(g * WIDTH, WIDTH)
        return (
            pltpu.make_async_copy(o_hbm.at[:, cols], o_ref.at[g], in_sem.at[g, 0]),
            pltpu.make_async_copy(d_hbm.at[:, cols], d_ref.at[g], in_sem.at[g, 1]),
        )

    for g in order:
        for copy in load(g):
            copy.start()

    def remote(src, dst, sem, where):
        return pltpu.make_async_remote_copy(
            src_ref=src,
            dst_ref=dst,
            send_sem=sem.at[0],
            recv_sem=sem.at[1],
            device_id=where,
            device_id_type=mesh_id,
        )

    barrier = pltpu.get_barrier_semaphore()
    pl.semaphore_signal(barrier, inc=1, device_id=core, device_id_type=mesh_id)
    pl.semaphore_signal(barrier, inc=1, device_id=beside, device_id_type=mesh_id)

    @pl.when(has_up)
    def _():
        for m in range(2):
            both = {"var": b + 2, "samp": m}
            pl.semaphore_signal(barrier, inc=1, device_id=both, device_id_type=mesh_id)

    @pl.when(has_down)
    def _():
        for m in range(2):
            both = {"var": b - 2, "samp": m}
            pl.semaphore_signal(barrier, inc=1, device_id=both, device_id_type=mesh_id)

    def fold(x):
        return jnp.sum(x.reshape(folds, 8, x.shape[-1]), axis=0)

    def block_rows(r):
        return pl.ds(pl.multiple_of(r * ROWS, ROWS), ROWS)

    def read(g, r, cols):
        present = o_ref[g, block_rows(r), cols].astype(jnp.float32)
        return present, d_ref[g, block_rows(r), cols].astype(jnp.float32)

    stat_mine[...] = jnp.zeros_like(stat_mine)

    def sums(g):
        for copy in load(g):
            copy.wait()
        zero = jnp.zeros((8, WIDTH), jnp.float32)
        everything = slice(0, WIDTH)

        def first(r, carry):
            present, values = read(g, r, everything)
            return carry[0] + fold(present), carry[1] + fold(present * values)

        count8, sum8 = lax.fori_loop(0, steps, first, (zero, zero))
        count = jnp.sum(count8, axis=0, keepdims=True)
        summed = jnp.sum(sum8, axis=0, keepdims=True)
        mean = summed / jnp.maximum(count, 1.0)

        def second(r, carry):
            present, values = read(g, r, everything)
            off = present * (values - mean)
            return carry + fold(off * off)

        square = jnp.sum(lax.fori_loop(0, steps, second, zero), axis=0, keepdims=True)
        stat_mine[g, 0:1, :] = count
        stat_mine[g, 1:2, :] = summed
        stat_mine[g, 2:3, :] = square

    def stat_copy(g):
        return remote(stat_mine.at[g], stat_other.at[g], stat_sem.at[g], core)

    def score(g, who):
        cols = pl.ds(pl.multiple_of(who * LANES, LANES), LANES)
        n_a, n_b = stat_mine[g, 0:1, cols], stat_other[g, 0:1, cols]
        s_a, s_b = stat_mine[g, 1:2, cols], stat_other[g, 1:2, cols]
        count = jnp.maximum(n_a + n_b, 1.0)
        center = (s_a + s_b) / count
        gap_a = s_a / jnp.maximum(n_a, 1.0) - center
        gap_b = s_b / jnp.maximum(n_b, 1.0) - center
        square = (stat_mine[g, 2:3, cols] + n_a * gap_a * gap_a) + (
            stat_other[g, 2:3, cols] + n_b * gap_b * gap_b
        )
        scale = lax.rsqrt(square / count + epsilon)

        def third(r, carry):
            present, values = read(g, r, cols)
            out = (present * (values - center) * scale).astype(jnp.bfloat16)
            s0[g, who, pl.ds(pl.multiple_of(c * local + r * ROWS, ROWS), ROWS), :] = out
            return carry

        lax.fori_loop(0, steps, third, 0)

    def part(ref, unit, who=c):
        g, st, first, count = unit
        start = pl.multiple_of(who * local + first * piece, piece)
        return ref.at[g, st, pl.ds(start, count * piece), :]

    def samples_copy(g, who):
        ref = s0.at[g, :, pl.ds(pl.multiple_of(who * local, local), local), :]
        return remote(ref, ref, own_sem.at[g], core)

    def down_copy(u):
        unit = down_units[u]
        return remote(part(s0, unit), part(s2, unit), down_sem.at[u], below)

    def down_got(u):
        ref = part(s2, down_units[u])
        return remote(ref, ref, down_sem.at[u], above)

    def relay_copy(u):
        unit = down_units[u]
        return remote(part(s2, unit), part(s1, unit), relay_sem.at[u], beside)

    def relay_got(u):
        ref = part(s1, down_units[u])
        return remote(ref, ref, relay_sem.at[u], beside)

    def y_copy(g, st):
        unit = (g, st, 0, SPLIT)
        return remote(part(s0, unit), part(s1, unit), y_sem.at[g, st], beside)

    def y_got(g, st):
        ref = part(s1, (g, st, 0, SPLIT))
        return remote(ref, ref, y_sem.at[g, st], beside)

    def round_copy(leg, u):
        unit = round_units[u]
        src, dst, where = ((s0, s2, beside), (s2, s1, below), (s1, s2, beside))[leg]
        return remote(part(src, unit), part(dst, unit), round_sem.at[leg, u], where)

    def round_got(leg, u):
        ref = part((s2, s1, s2)[leg], round_units[u])
        return remote(ref, ref, round_sem.at[leg, u], above if leg == 1 else beside)

    kept = (order[1], 0, 0, SPLIT)
    after_first = pl.ds(LANES, r2s.shape[1] - LANES)

    def ahead_copy():
        return remote(part(s0, (0, 0, 0, SPLIT)), part(s2, kept), ahead_sem.at[0], below)

    def ahead_got():
        return remote(part(s2, kept), part(s2, kept), ahead_sem.at[0], above)

    def ahead_across(mine):
        ref = part(s2, kept, c if mine else 1 - c)
        return remote(ref, ref, ahead_sem.at[1], core)

    transit = jnp.logical_and(odd, has_down)

    def send_stripe(g, st):
        @pl.when(jnp.logical_and(even, has_down))
        def _():
            for u, unit in enumerate(down_units):
                if unit[:2] == (g, st):
                    down_copy(u).start()
            for u, unit in enumerate(round_units):
                if unit[:2] == (g, st):
                    round_copy(0, u).start()

        @pl.when(odd)
        def _():
            y_copy(g, st).start()

        if (g, st) == stripes[0]:

            @pl.when(transit)
            def _():
                ahead_copy().start()

    def pass_down(u):
        round_got(0, u).wait_recv()
        round_copy(1, u).start()

    def up_copy(k):
        rows = pl.ds(k * TURNED, TURNED)
        return remote(tu.at[rows, :], tm.at[rows, :], up_sem.at[k], above)

    def up_got(k):
        ref = tm.at[pl.ds(k * TURNED, TURNED), :]
        return remote(ref, ref, up_sem.at[k], below)

    def finish(g):
        for st in range(2):
            score(g, st)
            send_stripe(g, st)
        samples_copy(g, c).start()

    def complete(i):
        g = order[i]
        samples_copy(g, 1 - c).wait_recv()

        @pl.when(has_up)
        def _():
            for q in range(4):
                rows = slice(q * (full // 4), (q + 1) * (full // 4))
                tu[i * LANES : (i + 1) * LANES, rows] = s0[g, c, rows, :].T
            for k in range(i * (LANES // TURNED), (i + 1) * (LANES // TURNED)):
                up_copy(k).start()

    def turn_own():
        def one(r, carry):
            for st in range(2):
                for q in range(4):
                    rows = slice(q * (full // 4), (q + 1) * (full // 4))
                    at = pl.multiple_of(r * WIDTH + st * LANES, LANES)
                    t0[pl.ds(at, LANES), rows] = s0[c * (groups // 2) + r, st, rows, :].T
            return carry

        lax.fori_loop(0, groups // 2, one, 0)

    def pass_some(units):
        @pl.when(transit)
        def _():
            for u in units:
                if u < len(round_units):
                    pass_down(u)

    sums(order[0])
    pl.semaphore_wait(barrier, 2 + 2 * (has_up.astype(jnp.int32) + has_down.astype(jnp.int32)))
    stat_copy(order[0]).start()
    sums(order[1])
    stat_copy(order[1]).start()
    for i, g in enumerate(order):
        stat_copy(g).wait()
        finish(g)
        if i > 0:
            complete(i - 1)
            pass_some((2 * i - 2, 2 * i - 1))
        if i > 0 and i + 1 < groups:
            sums(order[i + 1])
            stat_copy(order[i + 1]).start()
    complete(groups - 1)
    turn_own()

    def right(s, g):
        return jnp.concatenate([s[g, 0], s[g, 1]], axis=1)

    def column(g):
        start = g * WIDTH
        return pl.ds(start if isinstance(g, int) else pl.multiple_of(start, WIDTH), WIDTH)

    def product(left, s, g):
        acc = jnp.dot(left, right(s, g), preferred_element_type=jnp.float32)
        return (acc * (1.0 / total)).astype(jnp.bfloat16)

    def tile(k, s, g):
        obuf[k, :, column(g)] = product(t0[...], s, g)

    def tile_range(k, s, lo, hi):
        def one(g, carry):
            tile(k, s, g)
            return carry

        lax.fori_loop(lo, hi, one, 0)

    def ahead_store():
        cols = pl.ds(0, LANES)
        return pltpu.make_async_copy(obuf.at[2, :, cols], out_ref.at[2, :, cols], out_sem.at[2])

    def store(k):
        return pltpu.make_async_copy(obuf.at[k], out_ref.at[k], out_sem.at[k])

    def x1_copy(g, st, mine):
        ref = part(s1, (g, st, 0, SPLIT), c if mine else 1 - c)
        return remote(ref, ref, x1_sem.at[g, st], core)

    def x2_copy(u, mine):
        ref = part(s2, (down_units + round_units)[u], c if mine else 1 - c)
        return remote(ref, ref, x2_sem.at[u], core)

    def behind_to(start, size, k, cols):
        i = start // LANES
        at = (i // 2) * WIDTH + c * LANES + lax.rem(start, LANES)
        rows = pl.ds(pl.multiple_of(at, TURNED), size)
        return out_ref.at[k, rows, cols], {"var": b - 2, "samp": lax.rem(i, 2)}

    def r3_stripe(k, g, st):
        start = pl.multiple_of(k * TURNED, TURNED)
        rows = pl.ds(start, TURNED)
        cols = pl.ds(st * LANES, LANES)
        acc = jnp.dot(tm[rows, :], s1[g, st], preferred_element_type=jnp.float32)
        r3s[g, rows, cols] = (acc * (1.0 / total)).astype(jnp.bfloat16)
        dst, where = behind_to(start, TURNED, WIN - 1, pl.ds(g * WIDTH + st * LANES, LANES))
        remote(r3s.at[g, rows, cols], dst, r3_sem, where).start()

    def r3_group(k, g):
        start = pl.multiple_of(k * TURNED, TURNED)
        rows = pl.ds(start, TURNED)
        r3s[g, rows, :] = product(tm[rows, :], s1, g)
        dst, where = behind_to(start, TURNED, WIN - 1, column(g))
        remote(r3s.at[g, rows, :], dst, r3_sem, where).start()

    def r3_row(k, count):
        for j in range(count // 2):
            r3_group(jnp.int32(k), order[j])
        if count % 2:
            r3_stripe(jnp.int32(k), *stripes[count - 1])

    def r2_odd(k):
        rows = pl.ds(k * TURNED, TURNED)

        def one(g, carry):
            r2s[rows, column(g)] = product(tm[rows, :], s0, g)
            return carry

        lax.fori_loop(0, groups, one, 0)
        dst, where = behind_to(jnp.int32(k * TURNED), TURNED, WIN - 2, after_first)
        remote(r2s.at[rows, after_first], dst, r2_sem, where).start()

    def over(lo, hi, body):
        def one(r, carry):
            body(r)
            return carry

        lax.fori_loop(lo, hi, one, 0)

    def drain_common():
        for g in range(groups):
            samples_copy(g, c).wait_send()

        @pl.when(has_up)
        def _():
            for k in range(rows_out // TURNED):
                up_copy(k).wait_send()

        @pl.when(jnp.logical_or(even, has_up))
        def _():
            for g, st in stripes:
                x1_copy(g, st, True).wait_send()

    def sent_results(buffer, sem):
        remote(buffer, buffer, sem, below).wait_send()

    def got_results(k, sem):
        ref = out_ref.at[k, :, after_first] if k == WIN - 2 else out_ref.at[k]
        remote(ref, ref, sem, above).wait_recv()

    @pl.when(even)
    def _():
        def relay(u):
            @pl.when(has_up)
            def _():
                down_got(u).wait_recv()
                relay_copy(u).start()
                x2_copy(u, True).start()

        def second(i):
            @pl.when(has_up)
            def _():
                for u, unit in enumerate(down_units):
                    if unit[0] == order[i]:
                        x2_copy(u, False).wait_recv()
                tile(2, s2, order[i])

        relay(0)
        tile_range(0, s0, 0, groups)
        store(0).start()
        for j, (g, st) in enumerate(stripes):
            y_got(g, st).wait_recv()
            x1_copy(g, st, True).start()
            if j + 1 < len(down_units):
                relay(j + 1)
            x1_copy(g, st, False).wait_recv()

            @pl.when(has_down)
            def _():
                over(0, j, lambda k: r3_stripe(k, g, st))
                up_got(j).wait_recv()
                r3_row(j, j + 1)

            if st == 1:
                tile(1, s1, g)
                if g != order[0]:
                    second(order.index(g))
        store(1).start()
        drain_common()

        @pl.when(has_down)
        def _():
            for v in range(len(down_units)):
                down_copy(v).wait_send()
            for v in range(len(round_units)):
                round_copy(0, v).wait_send()

        @pl.when(has_up)
        def _():
            for v in range(len(down_units)):
                relay_copy(v).wait_send()
                x2_copy(v, True).wait_send()
            for v, unit in enumerate(down_units):
                if unit[0] == 0:
                    x2_copy(v, False).wait_recv()
            for v in range(len(round_units)):
                round_got(2, v).wait_recv()
                x2_copy(len(down_units) + v, True).start()
            for v in range(len(round_units)):
                x2_copy(len(down_units) + v, False).wait_recv()
            tile(2, s2, 0)
            store(2).start()
            for v in range(len(round_units)):
                x2_copy(len(down_units) + v, True).wait_send()

        @pl.when(has_down)
        def _():
            sent_results(r3s, r3_sem)

        @pl.when(has_up)
        def _():
            got_results(WIN - 1, r3_sem)
            store(2).wait()

    @pl.when(odd)
    def _():
        def turn(k, count):
            @pl.when(has_down)
            def _():
                up_got(k).wait_recv()
                r2_odd(k)

            @pl.when(jnp.logical_and(has_down, has_up))
            def _():
                r3_row(k, count)

        def arrive(j):
            g, st = stripes[j]

            @pl.when(has_up)
            def _():
                for v, unit in enumerate(round_units):
                    if unit[:2] == (g, st):
                        round_got(1, v).wait_recv()
                        round_copy(2, v).start()
                for v, unit in enumerate(down_units):
                    if unit[:2] == (g, st):
                        relay_got(v).wait_recv()
                x1_copy(g, st, True).start()

        def column_of(j, rows):
            g, st = stripes[j]

            @pl.when(has_up)
            def _():
                x1_copy(g, st, False).wait_recv()

            @pl.when(jnp.logical_and(has_down, has_up))
            def _():
                over(0, rows, lambda k: r3_stripe(k, g, st))

        def first(i):
            @pl.when(has_up)
            def _():
                tile(1, s1, order[i])

        turn(0, 0)

        @pl.when(has_down)
        def _():
            for u in range(2 * groups - 2, len(round_units)):
                pass_down(u)

        tile_range(0, s0, 0, groups)
        store(0).start()

        @pl.when(has_up)
        def _():
            ahead_got().wait_recv()
            ahead_across(True).start()

        arrive(0)
        turn(1, 0)
        arrive(1)
        column_of(0, 2)
        column_of(1, 2)
        for k in range(2, len(stripes)):
            arrive(k)
            turn(k, k)
            column_of(k, k + 1)
            if k % 2 == 0:
                first(k // 2 - 1)
            if k == 3:

                @pl.when(has_up)
                def _():
                    ahead_across(False).wait_recv()
                    acc = jnp.dot(t0[...], s2[kept[0], 0], preferred_element_type=jnp.float32)
                    obuf[2, :, 0:LANES] = (acc * (1.0 / total)).astype(jnp.bfloat16)
                    ahead_store().start()

        first(groups - 1)
        store(1).start()
        drain_common()
        for g in range(groups):
            for h in range(2):
                y_copy(g, h).wait_send()

        @pl.when(has_down)
        def _():
            for v in range(len(round_units)):
                round_copy(1, v).wait_send()

        @pl.when(has_up)
        def _():
            for v in range(len(round_units)):
                round_copy(2, v).wait_send()

        @pl.when(has_down)
        def _():
            sent_results(r2s.at[:, after_first], r2_sem)
            ahead_copy().wait_send()

        @pl.when(jnp.logical_and(has_down, has_up))
        def _():
            sent_results(r3s, r3_sem)

        @pl.when(has_up)
        def _():
            got_results(WIN - 2, r2_sem)
            ahead_across(True).wait_send()
            ahead_store().wait()

        @pl.when(b + 4 < n)
        def _():
            got_results(WIN - 1, r3_sem)

    store(0).wait()
    store(1).wait()


def per_device(dosage, observed, counts):
    local, variants = dosage.shape
    n = lax.axis_size("var")
    full = local * lax.axis_size("samp")
    half = variants // 2
    groups = variants // WIDTH
    downs = len(STRAIGHT) + 2 * (groups - 1)
    rounds = len(ROUND)
    dma = pltpu.SemaphoreType.DMA
    block = pltpu.VMEM((groups, 2, full, LANES), jnp.bfloat16)
    tiles = pl.pallas_call(
        functools.partial(kernel, n, float(full)),
        out_shape=jax.ShapeDtypeStruct((WIN, half, variants), jnp.bfloat16),
        in_specs=[pl.BlockSpec(memory_space=pltpu.HBM)] * 2,
        out_specs=pl.BlockSpec(memory_space=pl.ANY),
        scratch_shapes=[
            pltpu.VMEM((groups, local, WIDTH), dosage.dtype),
            pltpu.VMEM((groups, local, WIDTH), observed.dtype),
            block,
            block,
            block,
            pltpu.VMEM((half, full), jnp.bfloat16),
            pltpu.VMEM((half, full), jnp.bfloat16),
            pltpu.VMEM((half, full), jnp.bfloat16),
            pltpu.VMEM((half, variants), jnp.bfloat16),
            pltpu.VMEM((groups, half, WIDTH), jnp.bfloat16),
            pltpu.VMEM((groups, 8, WIDTH), jnp.float32),
            pltpu.VMEM((groups, 8, WIDTH), jnp.float32),
            pltpu.VMEM((WIN - 1, half, variants), jnp.bfloat16),
            dma((groups, 2)),
            dma((groups, 2)),
            dma((groups, 2)),
            dma((downs, 2)),
            dma((downs, 2)),
            dma((groups, 2, 2)),
            dma((half // TURNED, 2)),
            dma((3, max(rounds, 1), 2)),
            dma((groups, 2, 2)),
            dma((downs + rounds, 2)),
            dma((2,)),
            dma((2,)),
            dma((2, 2)),
            dma((WIN - 1,)),
        ],
        compiler_params=pltpu.CompilerParams(
            collective_id=0, has_side_effects=True, vmem_limit_bytes=VMEM_LIMIT
        ),
    )(
        pltpu.with_memory_space_constraint(dosage, pltpu.HBM),
        pltpu.with_memory_space_constraint(observed, pltpu.HBM),
    )
    keep = jnp.arange(WIN, dtype=jnp.int32)[:, None, None] < counts[0]
    return jnp.where(keep, tiles, jnp.zeros_like(tiles))[None]


def solution(mesh):
    in_specs = (P("samp", ("region", "var")), P("samp", ("region", "var")), P(("region", "var")))
    out_specs = P(("region", "var"), None, "samp", None)
    return jax.shard_map(
        per_device, mesh=mesh, in_specs=in_specs, out_specs=out_specs, check_vma=False
    )
```

```python
import functools

import jax
import jax.numpy as jnp
from jax import lax
from jax.experimental import pallas as pl
from jax.experimental.pallas import tpu as pltpu
from jax.sharding import PartitionSpec as P

WIN = 4

epsilon = 1e-05

LANES = 128
WIDTH = 2 * LANES
ROWS = 128
SPLIT = 8
TURNED = 64
STRAIGHT = ((1, 5, 3),)
ROUND = ((0, 0, 2), (0, 2, 2), (0, 4, 2), (0, 6, 2), (1, 0, 2), (1, 2, 2), (1, 4, 1))
VMEM_LIMIT = 40 * 1024 * 1024


def kernel(
    n,
    total,
    d_hbm,
    o_hbm,
    out_ref,
    d_ref,
    o_ref,
    s0,
    s1,
    s2,
    t0,
    tu,
    tm,
    r2s,
    r3s,
    stat_mine,
    stat_other,
    obuf,
    in_sem,
    stat_sem,
    own_sem,
    down_sem,
    relay_sem,
    y_sem,
    up_sem,
    round_sem,
    x1_sem,
    x2_sem,
    r2_sem,
    r3_sem,
    ahead_sem,
    out_sem,
):
    b = lax.axis_index("var")
    c = lax.axis_index("samp")
    even = lax.rem(b, 2) == 0
    odd = jnp.logical_not(even)
    pair = b + 1 - 2 * lax.rem(b, 2)
    has_up = b + 2 < n
    has_down = b >= 2
    core = {"samp": 1 - c}
    below, above, beside = {"var": b - 2}, {"var": b + 2}, {"var": pair}
    groups, _, full, _ = s0.shape
    local = full // 2
    rows_out = t0.shape[0]
    steps = local // ROWS
    folds = ROWS // 8
    piece = local // SPLIT
    mesh_id = pl.DeviceIdType.MESH
    order = [g for r in range(groups // 2) for g in (r, groups // 2 + r)]
    stripes = [(g, st) for g in order for st in range(2)]
    down_units = [(0, st, p, k) for st, p, k in STRAIGHT] + [(g, st, 0, SPLIT) for g, st in stripes[2:]]
    round_units = [(0, st, p, k) for st, p, k in ROUND]

    def load(g):
        cols = pl.ds(g * WIDTH, WIDTH)
        return (
            pltpu.make_async_copy(o_hbm.at[:, cols], o_ref.at[g], in_sem.at[g, 0]),
            pltpu.make_async_copy(d_hbm.at[:, cols], d_ref.at[g], in_sem.at[g, 1]),
        )

    for g in order:
        for copy in load(g):
            copy.start()

    def remote(src, dst, sem, where):
        return pltpu.make_async_remote_copy(
            src_ref=src,
            dst_ref=dst,
            send_sem=sem.at[0],
            recv_sem=sem.at[1],
            device_id=where,
            device_id_type=mesh_id,
        )

    barrier = pltpu.get_barrier_semaphore()
    pl.semaphore_signal(barrier, inc=1, device_id=core, device_id_type=mesh_id)
    pl.semaphore_signal(barrier, inc=1, device_id=beside, device_id_type=mesh_id)

    @pl.when(has_up)
    def _():
        for m in range(2):
            both = {"var": b + 2, "samp": m}
            pl.semaphore_signal(barrier, inc=1, device_id=both, device_id_type=mesh_id)

    @pl.when(has_down)
    def _():
        for m in range(2):
            both = {"var": b - 2, "samp": m}
            pl.semaphore_signal(barrier, inc=1, device_id=both, device_id_type=mesh_id)

    def fold(x):
        return jnp.sum(x.reshape(folds, 8, x.shape[-1]), axis=0)

    def block_rows(r):
        return pl.ds(pl.multiple_of(r * ROWS, ROWS), ROWS)

    def read(g, r, cols):
        present = o_ref[g, block_rows(r), cols].astype(jnp.float32)
        return present, d_ref[g, block_rows(r), cols].astype(jnp.float32)

    stat_mine[...] = jnp.zeros_like(stat_mine)

    def sums(g):
        for copy in load(g):
            copy.wait()
        zero = jnp.zeros((8, WIDTH), jnp.float32)
        everything = slice(0, WIDTH)

        def first(r, carry):
            present, values = read(g, r, everything)
            return carry[0] + fold(present), carry[1] + fold(present * values)

        count8, sum8 = lax.fori_loop(0, steps, first, (zero, zero))
        count = jnp.sum(count8, axis=0, keepdims=True)
        summed = jnp.sum(sum8, axis=0, keepdims=True)
        mean = summed / jnp.maximum(count, 1.0)

        def second(r, carry):
            present, values = read(g, r, everything)
            off = present * (values - mean)
            return carry + fold(off * off)

        square = jnp.sum(lax.fori_loop(0, steps, second, zero), axis=0, keepdims=True)
        stat_mine[g, 0:1, :] = count
        stat_mine[g, 1:2, :] = summed
        stat_mine[g, 2:3, :] = square

    def stat_copy(g):
        return remote(stat_mine.at[g], stat_other.at[g], stat_sem.at[g], core)

    def score(g, who):
        cols = pl.ds(pl.multiple_of(who * LANES, LANES), LANES)
        n_a, n_b = stat_mine[g, 0:1, cols], stat_other[g, 0:1, cols]
        s_a, s_b = stat_mine[g, 1:2, cols], stat_other[g, 1:2, cols]
        count = jnp.maximum(n_a + n_b, 1.0)
        center = (s_a + s_b) / count
        gap_a = s_a / jnp.maximum(n_a, 1.0) - center
        gap_b = s_b / jnp.maximum(n_b, 1.0) - center
        square = (stat_mine[g, 2:3, cols] + n_a * gap_a * gap_a) + (
            stat_other[g, 2:3, cols] + n_b * gap_b * gap_b
        )
        scale = lax.rsqrt(square / count + epsilon)

        def third(r, carry):
            present, values = read(g, r, cols)
            out = (present * (values - center) * scale).astype(jnp.bfloat16)
            s0[g, who, pl.ds(pl.multiple_of(c * local + r * ROWS, ROWS), ROWS), :] = out
            return carry

        lax.fori_loop(0, steps, third, 0)

    def part(ref, unit, who=c):
        g, st, first, count = unit
        start = pl.multiple_of(who * local + first * piece, piece)
        return ref.at[g, st, pl.ds(start, count * piece), :]

    def samples_copy(g, who):
        ref = s0.at[g, :, pl.ds(pl.multiple_of(who * local, local), local), :]
        return remote(ref, ref, own_sem.at[g], core)

    def down_copy(u):
        unit = down_units[u]
        return remote(part(s0, unit), part(s2, unit), down_sem.at[u], below)

    def down_got(u):
        ref = part(s2, down_units[u])
        return remote(ref, ref, down_sem.at[u], above)

    def relay_copy(u):
        unit = down_units[u]
        return remote(part(s2, unit), part(s1, unit), relay_sem.at[u], beside)

    def relay_got(u):
        ref = part(s1, down_units[u])
        return remote(ref, ref, relay_sem.at[u], beside)

    def y_copy(g, st):
        unit = (g, st, 0, SPLIT)
        return remote(part(s0, unit), part(s1, unit), y_sem.at[g, st], beside)

    def y_got(g, st):
        ref = part(s1, (g, st, 0, SPLIT))
        return remote(ref, ref, y_sem.at[g, st], beside)

    def round_copy(leg, u):
        unit = round_units[u]
        src, dst, where = ((s0, s2, beside), (s2, s1, below), (s1, s2, beside))[leg]
        return remote(part(src, unit), part(dst, unit), round_sem.at[leg, u], where)

    def round_got(leg, u):
        ref = part((s2, s1, s2)[leg], round_units[u])
        return remote(ref, ref, round_sem.at[leg, u], above if leg == 1 else beside)

    kept = (order[1], 0, 0, SPLIT)
    after_first = pl.ds(LANES, r2s.shape[1] - LANES)

    def ahead_copy():
        return remote(part(s0, (0, 0, 0, SPLIT)), part(s2, kept), ahead_sem.at[0], below)

    def ahead_got():
        return remote(part(s2, kept), part(s2, kept), ahead_sem.at[0], above)

    def ahead_across(mine):
        ref = part(s2, kept, c if mine else 1 - c)
        return remote(ref, ref, ahead_sem.at[1], core)

    transit = jnp.logical_and(odd, has_down)

    def send_stripe(g, st):
        @pl.when(jnp.logical_and(even, has_down))
        def _():
            for u, unit in enumerate(down_units):
                if unit[:2] == (g, st):
                    down_copy(u).start()
            for u, unit in enumerate(round_units):
                if unit[:2] == (g, st):
                    round_copy(0, u).start()

        @pl.when(odd)
        def _():
            y_copy(g, st).start()

        if (g, st) == stripes[0]:

            @pl.when(transit)
            def _():
                ahead_copy().start()

    def pass_down(u):
        round_got(0, u).wait_recv()
        round_copy(1, u).start()

    def up_copy(k):
        rows = pl.ds(k * TURNED, TURNED)
        return remote(tu.at[rows, :], tm.at[rows, :], up_sem.at[k], above)

    def up_got(k):
        ref = tm.at[pl.ds(k * TURNED, TURNED), :]
        return remote(ref, ref, up_sem.at[k], below)

    def finish(g):
        for st in range(2):
            score(g, st)
            send_stripe(g, st)
        samples_copy(g, c).start()

    def complete(i):
        g = order[i]
        samples_copy(g, 1 - c).wait_recv()

        @pl.when(has_up)
        def _():
            for q in range(4):
                rows = slice(q * (full // 4), (q + 1) * (full // 4))
                tu[i * LANES : (i + 1) * LANES, rows] = s0[g, c, rows, :].T
            for k in range(i * (LANES // TURNED), (i + 1) * (LANES // TURNED)):
                up_copy(k).start()

    def turn_own():
        def one(r, carry):
            for st in range(2):
                for q in range(4):
                    rows = slice(q * (full // 4), (q + 1) * (full // 4))
                    at = pl.multiple_of(r * WIDTH + st * LANES, LANES)
                    t0[pl.ds(at, LANES), rows] = s0[c * (groups // 2) + r, st, rows, :].T
            return carry

        lax.fori_loop(0, groups // 2, one, 0)

    def pass_some(units):
        @pl.when(transit)
        def _():
            for u in units:
                if u < len(round_units):
                    pass_down(u)

    sums(order[0])
    pl.semaphore_wait(barrier, 2 + 2 * (has_up.astype(jnp.int32) + has_down.astype(jnp.int32)))
    stat_copy(order[0]).start()
    sums(order[1])
    stat_copy(order[1]).start()
    for i, g in enumerate(order):
        stat_copy(g).wait()
        finish(g)
        if i > 0:
            complete(i - 1)
            pass_some(((), (), (0, 1), (2, 3))[i])
        if i > 0 and i + 1 < groups:
            sums(order[i + 1])
            stat_copy(order[i + 1]).start()
    complete(groups - 1)
    pass_some((4, 5))
    turn_own()

    def right(s, g):
        return jnp.concatenate([s[g, 0], s[g, 1]], axis=1)

    def column(g):
        start = g * WIDTH
        return pl.ds(start if isinstance(g, int) else pl.multiple_of(start, WIDTH), WIDTH)

    def product(left, s, g):
        acc = jnp.dot(left, right(s, g), preferred_element_type=jnp.float32)
        return (acc * (1.0 / total)).astype(jnp.bfloat16)

    def tile(k, s, g):
        obuf[k, :, column(g)] = product(t0[...], s, g)

    def tile_range(k, s, lo, hi):
        def one(g, carry):
            tile(k, s, g)
            return carry

        lax.fori_loop(lo, hi, one, 0)

    def ahead_store():
        cols = pl.ds(0, LANES)
        return pltpu.make_async_copy(obuf.at[2, :, cols], out_ref.at[2, :, cols], out_sem.at[2])

    def store(k):
        return pltpu.make_async_copy(obuf.at[k], out_ref.at[k], out_sem.at[k])

    def x1_copy(g, st, mine):
        ref = part(s1, (g, st, 0, SPLIT), c if mine else 1 - c)
        return remote(ref, ref, x1_sem.at[g, st], core)

    def x2_copy(u, mine):
        ref = part(s2, (down_units + round_units)[u], c if mine else 1 - c)
        return remote(ref, ref, x2_sem.at[u], core)

    def behind_to(start, size, k, cols):
        i = start // LANES
        at = (i // 2) * WIDTH + c * LANES + lax.rem(start, LANES)
        rows = pl.ds(pl.multiple_of(at, TURNED), size)
        return out_ref.at[k, rows, cols], {"var": b - 2, "samp": lax.rem(i, 2)}

    def r3_stripe(k, g, st):
        start = pl.multiple_of(k * TURNED, TURNED)
        rows = pl.ds(start, TURNED)
        cols = pl.ds(st * LANES, LANES)
        acc = jnp.dot(tm[rows, :], s1[g, st], preferred_element_type=jnp.float32)
        r3s[g, rows, cols] = (acc * (1.0 / total)).astype(jnp.bfloat16)
        dst, where = behind_to(start, TURNED, WIN - 1, pl.ds(g * WIDTH + st * LANES, LANES))
        remote(r3s.at[g, rows, cols], dst, r3_sem, where).start()

    def r3_group(k, g):
        start = pl.multiple_of(k * TURNED, TURNED)
        rows = pl.ds(start, TURNED)
        r3s[g, rows, :] = product(tm[rows, :], s1, g)
        dst, where = behind_to(start, TURNED, WIN - 1, column(g))
        remote(r3s.at[g, rows, :], dst, r3_sem, where).start()

    def r3_row(k, count):
        for j in range(count // 2):
            r3_group(jnp.int32(k), order[j])
        if count % 2:
            r3_stripe(jnp.int32(k), *stripes[count - 1])

    def r2_odd(k):
        rows = pl.ds(k * TURNED, TURNED)

        def one(g, carry):
            r2s[rows, column(g)] = product(tm[rows, :], s0, g)
            return carry

        lax.fori_loop(0, groups, one, 0)
        dst, where = behind_to(jnp.int32(k * TURNED), TURNED, WIN - 2, after_first)
        remote(r2s.at[rows, after_first], dst, r2_sem, where).start()

    def over(lo, hi, body):
        def one(r, carry):
            body(r)
            return carry

        lax.fori_loop(lo, hi, one, 0)

    def drain_common():
        for g in range(groups):
            samples_copy(g, c).wait_send()

        @pl.when(has_up)
        def _():
            for k in range(rows_out // TURNED):
                up_copy(k).wait_send()

        @pl.when(jnp.logical_or(even, has_up))
        def _():
            for g, st in stripes:
                x1_copy(g, st, True).wait_send()

    def sent_results(buffer, sem):
        remote(buffer, buffer, sem, below).wait_send()

    def got_results(k, sem):
        ref = out_ref.at[k, :, after_first] if k == WIN - 2 else out_ref.at[k]
        remote(ref, ref, sem, above).wait_recv()

    @pl.when(even)
    def _():
        def relay(u):
            @pl.when(has_up)
            def _():
                down_got(u).wait_recv()
                relay_copy(u).start()
                x2_copy(u, True).start()

        def second(i):
            @pl.when(has_up)
            def _():
                for u, unit in enumerate(down_units):
                    if unit[0] == order[i]:
                        x2_copy(u, False).wait_recv()
                tile(2, s2, order[i])

        relay(0)
        tile_range(0, s0, 0, groups)
        store(0).start()
        for j, (g, st) in enumerate(stripes):
            y_got(g, st).wait_recv()
            x1_copy(g, st, True).start()
            if j + 1 < len(down_units):
                relay(j + 1)
            x1_copy(g, st, False).wait_recv()

            @pl.when(has_down)
            def _():
                over(0, j, lambda k: r3_stripe(k, g, st))
                up_got(j).wait_recv()
                r3_row(j, j + 1)

            if st == 1:
                tile(1, s1, g)
                if g != order[0]:
                    second(order.index(g))
        store(1).start()
        drain_common()

        @pl.when(has_down)
        def _():
            for v in range(len(down_units)):
                down_copy(v).wait_send()
            for v in range(len(round_units)):
                round_copy(0, v).wait_send()

        @pl.when(has_up)
        def _():
            for v in range(len(down_units)):
                relay_copy(v).wait_send()
                x2_copy(v, True).wait_send()
            for v, unit in enumerate(down_units):
                if unit[0] == 0:
                    x2_copy(v, False).wait_recv()
            for v in range(len(round_units)):
                round_got(2, v).wait_recv()
                x2_copy(len(down_units) + v, True).start()
            for v in range(len(round_units)):
                x2_copy(len(down_units) + v, False).wait_recv()
            tile(2, s2, 0)
            store(2).start()
            for v in range(len(round_units)):
                x2_copy(len(down_units) + v, True).wait_send()

        @pl.when(has_down)
        def _():
            sent_results(r3s, r3_sem)

        @pl.when(has_up)
        def _():
            got_results(WIN - 1, r3_sem)
            store(2).wait()

    @pl.when(odd)
    def _():
        def turn(k, count):
            @pl.when(has_down)
            def _():
                up_got(k).wait_recv()
                r2_odd(k)

            @pl.when(jnp.logical_and(has_down, has_up))
            def _():
                r3_row(k, count)

        def arrive(j):
            g, st = stripes[j]

            @pl.when(has_up)
            def _():
                for v, unit in enumerate(round_units):
                    if unit[:2] == (g, st):
                        round_got(1, v).wait_recv()
                        round_copy(2, v).start()
                for v, unit in enumerate(down_units):
                    if unit[:2] == (g, st):
                        relay_got(v).wait_recv()
                x1_copy(g, st, True).start()

        def column_of(j, rows):
            g, st = stripes[j]

            @pl.when(has_up)
            def _():
                x1_copy(g, st, False).wait_recv()

            @pl.when(jnp.logical_and(has_down, has_up))
            def _():
                over(0, rows, lambda k: r3_stripe(k, g, st))

        def first(i):
            @pl.when(has_up)
            def _():
                tile(1, s1, order[i])

        turn(0, 0)

        @pl.when(has_down)
        def _():
            for u in range(2 * groups - 2, len(round_units)):
                pass_down(u)

        tile_range(0, s0, 0, groups)
        store(0).start()

        @pl.when(has_up)
        def _():
            ahead_got().wait_recv()
            ahead_across(True).start()

        arrive(0)
        turn(1, 0)
        arrive(1)
        column_of(0, 2)
        column_of(1, 2)
        for k in range(2, len(stripes)):
            arrive(k)
            turn(k, k)
            column_of(k, k + 1)
            if k % 2 == 0:
                first(k // 2 - 1)
            if k == 3:

                @pl.when(has_up)
                def _():
                    ahead_across(False).wait_recv()
                    acc = jnp.dot(t0[...], s2[kept[0], 0], preferred_element_type=jnp.float32)
                    obuf[2, :, 0:LANES] = (acc * (1.0 / total)).astype(jnp.bfloat16)
                    ahead_store().start()

        first(groups - 1)
        store(1).start()
        drain_common()
        for g in range(groups):
            for h in range(2):
                y_copy(g, h).wait_send()

        @pl.when(has_down)
        def _():
            for v in range(len(round_units)):
                round_copy(1, v).wait_send()

        @pl.when(has_up)
        def _():
            for v in range(len(round_units)):
                round_copy(2, v).wait_send()

        @pl.when(has_down)
        def _():
            sent_results(r2s.at[:, after_first], r2_sem)
            ahead_copy().wait_send()

        @pl.when(jnp.logical_and(has_down, has_up))
        def _():
            sent_results(r3s, r3_sem)

        @pl.when(has_up)
        def _():
            got_results(WIN - 2, r2_sem)
            ahead_across(True).wait_send()
            ahead_store().wait()

        @pl.when(b + 4 < n)
        def _():
            got_results(WIN - 1, r3_sem)

    store(0).wait()
    store(1).wait()


def per_device(dosage, observed, counts):
    local, variants = dosage.shape
    n = lax.axis_size("var")
    full = local * lax.axis_size("samp")
    half = variants // 2
    groups = variants // WIDTH
    downs = len(STRAIGHT) + 2 * (groups - 1)
    rounds = len(ROUND)
    dma = pltpu.SemaphoreType.DMA
    block = pltpu.VMEM((groups, 2, full, LANES), jnp.bfloat16)
    tiles = pl.pallas_call(
        functools.partial(kernel, n, float(full)),
        out_shape=jax.ShapeDtypeStruct((WIN, half, variants), jnp.bfloat16),
        in_specs=[pl.BlockSpec(memory_space=pltpu.HBM)] * 2,
        out_specs=pl.BlockSpec(memory_space=pl.ANY),
        scratch_shapes=[
            pltpu.VMEM((groups, local, WIDTH), dosage.dtype),
            pltpu.VMEM((groups, local, WIDTH), observed.dtype),
            block,
            block,
            block,
            pltpu.VMEM((half, full), jnp.bfloat16),
            pltpu.VMEM((half, full), jnp.bfloat16),
            pltpu.VMEM((half, full), jnp.bfloat16),
            pltpu.VMEM((half, variants), jnp.bfloat16),
            pltpu.VMEM((groups, half, WIDTH), jnp.bfloat16),
            pltpu.VMEM((groups, 8, WIDTH), jnp.float32),
            pltpu.VMEM((groups, 8, WIDTH), jnp.float32),
            pltpu.VMEM((WIN - 1, half, variants), jnp.bfloat16),
            dma((groups, 2)),
            dma((groups, 2)),
            dma((groups, 2)),
            dma((downs, 2)),
            dma((downs, 2)),
            dma((groups, 2, 2)),
            dma((half // TURNED, 2)),
            dma((3, max(rounds, 1), 2)),
            dma((groups, 2, 2)),
            dma((downs + rounds, 2)),
            dma((2,)),
            dma((2,)),
            dma((2, 2)),
            dma((WIN - 1,)),
        ],
        compiler_params=pltpu.CompilerParams(
            collective_id=0, has_side_effects=True, vmem_limit_bytes=VMEM_LIMIT
        ),
    )(
        pltpu.with_memory_space_constraint(dosage, pltpu.HBM),
        pltpu.with_memory_space_constraint(observed, pltpu.HBM),
    )
    keep = jnp.arange(WIN, dtype=jnp.int32)[:, None, None] < counts[0]
    return jnp.where(keep, tiles, jnp.zeros_like(tiles))[None]


def solution(mesh):
    in_specs = (P("samp", ("region", "var")), P("samp", ("region", "var")), P(("region", "var")))
    out_specs = P(("region", "var"), None, "samp", None)
    return jax.shard_map(
        per_device, mesh=mesh, in_specs=in_specs, out_specs=out_specs, check_vma=False
    )
```

```python
import functools

import jax
import jax.numpy as jnp
from jax import lax
from jax.experimental import pallas as pl
from jax.experimental.pallas import tpu as pltpu
from jax.sharding import PartitionSpec as P

WIN = 4

epsilon = 1e-05

LANES = 128
WIDTH = 2 * LANES
ROWS = 128
SPLIT = 8
TURNED = 64
STRAIGHT = ((1, 6, 2),)
ROUND = ((0, 0, 2), (0, 2, 2), (0, 4, 2), (0, 6, 2), (1, 0, 2), (1, 2, 2), (1, 4, 2))
VMEM_LIMIT = 40 * 1024 * 1024


def kernel(
    n,
    total,
    d_hbm,
    o_hbm,
    out_ref,
    d_ref,
    o_ref,
    s0,
    s1,
    s2,
    t0,
    tu,
    tm,
    r2s,
    r3s,
    stat_mine,
    stat_other,
    obuf,
    in_sem,
    stat_sem,
    own_sem,
    down_sem,
    relay_sem,
    y_sem,
    up_sem,
    round_sem,
    x1_sem,
    x2_sem,
    r2_sem,
    r3_sem,
    ahead_sem,
    out_sem,
):
    b = lax.axis_index("var")
    c = lax.axis_index("samp")
    even = lax.rem(b, 2) == 0
    odd = jnp.logical_not(even)
    pair = b + 1 - 2 * lax.rem(b, 2)
    has_up = b + 2 < n
    has_down = b >= 2
    core = {"samp": 1 - c}
    below, above, beside = {"var": b - 2}, {"var": b + 2}, {"var": pair}
    groups, _, full, _ = s0.shape
    local = full // 2
    rows_out = t0.shape[0]
    steps = local // ROWS
    folds = ROWS // 8
    piece = local // SPLIT
    mesh_id = pl.DeviceIdType.MESH
    order = [g for r in range(groups // 2) for g in (r, groups // 2 + r)]
    stripes = [(g, st) for g in order for st in range(2)]
    down_units = [(0, st, p, k) for st, p, k in STRAIGHT] + [(g, st, 0, SPLIT) for g, st in stripes[2:]]
    round_units = [(0, st, p, k) for st, p, k in ROUND]

    def load(g):
        cols = pl.ds(g * WIDTH, WIDTH)
        return (
            pltpu.make_async_copy(o_hbm.at[:, cols], o_ref.at[g], in_sem.at[g, 0]),
            pltpu.make_async_copy(d_hbm.at[:, cols], d_ref.at[g], in_sem.at[g, 1]),
        )

    for g in order:
        for copy in load(g):
            copy.start()

    def remote(src, dst, sem, where):
        return pltpu.make_async_remote_copy(
            src_ref=src,
            dst_ref=dst,
            send_sem=sem.at[0],
            recv_sem=sem.at[1],
            device_id=where,
            device_id_type=mesh_id,
        )

    barrier = pltpu.get_barrier_semaphore()
    pl.semaphore_signal(barrier, inc=1, device_id=core, device_id_type=mesh_id)
    pl.semaphore_signal(barrier, inc=1, device_id=beside, device_id_type=mesh_id)

    @pl.when(has_up)
    def _():
        for m in range(2):
            both = {"var": b + 2, "samp": m}
            pl.semaphore_signal(barrier, inc=1, device_id=both, device_id_type=mesh_id)

    @pl.when(has_down)
    def _():
        for m in range(2):
            both = {"var": b - 2, "samp": m}
            pl.semaphore_signal(barrier, inc=1, device_id=both, device_id_type=mesh_id)

    def fold(x):
        return jnp.sum(x.reshape(folds, 8, x.shape[-1]), axis=0)

    def block_rows(r):
        return pl.ds(pl.multiple_of(r * ROWS, ROWS), ROWS)

    def read(g, r, cols):
        present = o_ref[g, block_rows(r), cols].astype(jnp.float32)
        return present, d_ref[g, block_rows(r), cols].astype(jnp.float32)

    stat_mine[...] = jnp.zeros_like(stat_mine)

    def sums(g):
        for copy in load(g):
            copy.wait()
        zero = jnp.zeros((8, WIDTH), jnp.float32)
        everything = slice(0, WIDTH)

        def first(r, carry):
            present, values = read(g, r, everything)
            return carry[0] + fold(present), carry[1] + fold(present * values)

        count8, sum8 = lax.fori_loop(0, steps, first, (zero, zero))
        count = jnp.sum(count8, axis=0, keepdims=True)
        summed = jnp.sum(sum8, axis=0, keepdims=True)
        mean = summed / jnp.maximum(count, 1.0)

        def second(r, carry):
            present, values = read(g, r, everything)
            off = present * (values - mean)
            return carry + fold(off * off)

        square = jnp.sum(lax.fori_loop(0, steps, second, zero), axis=0, keepdims=True)
        stat_mine[g, 0:1, :] = count
        stat_mine[g, 1:2, :] = summed
        stat_mine[g, 2:3, :] = square

    def stat_copy(g):
        return remote(stat_mine.at[g], stat_other.at[g], stat_sem.at[g], core)

    def score(g, who):
        cols = pl.ds(pl.multiple_of(who * LANES, LANES), LANES)
        n_a, n_b = stat_mine[g, 0:1, cols], stat_other[g, 0:1, cols]
        s_a, s_b = stat_mine[g, 1:2, cols], stat_other[g, 1:2, cols]
        count = jnp.maximum(n_a + n_b, 1.0)
        center = (s_a + s_b) / count
        gap_a = s_a / jnp.maximum(n_a, 1.0) - center
        gap_b = s_b / jnp.maximum(n_b, 1.0) - center
        square = (stat_mine[g, 2:3, cols] + n_a * gap_a * gap_a) + (
            stat_other[g, 2:3, cols] + n_b * gap_b * gap_b
        )
        scale = lax.rsqrt(square / count + epsilon)

        def third(r, carry):
            present, values = read(g, r, cols)
            out = (present * (values - center) * scale).astype(jnp.bfloat16)
            s0[g, who, pl.ds(pl.multiple_of(c * local + r * ROWS, ROWS), ROWS), :] = out
            return carry

        lax.fori_loop(0, steps, third, 0)

    def part(ref, unit, who=c):
        g, st, first, count = unit
        start = pl.multiple_of(who * local + first * piece, piece)
        return ref.at[g, st, pl.ds(start, count * piece), :]

    def samples_copy(g, who):
        ref = s0.at[g, :, pl.ds(pl.multiple_of(who * local, local), local), :]
        return remote(ref, ref, own_sem.at[g], core)

    def down_copy(u):
        unit = down_units[u]
        return remote(part(s0, unit), part(s2, unit), down_sem.at[u], below)

    def down_got(u):
        ref = part(s2, down_units[u])
        return remote(ref, ref, down_sem.at[u], above)

    def relay_copy(u):
        unit = down_units[u]
        return remote(part(s2, unit), part(s1, unit), relay_sem.at[u], beside)

    def relay_got(u):
        ref = part(s1, down_units[u])
        return remote(ref, ref, relay_sem.at[u], beside)

    def y_copy(g, st):
        unit = (g, st, 0, SPLIT)
        return remote(part(s0, unit), part(s1, unit), y_sem.at[g, st], beside)

    def y_got(g, st):
        ref = part(s1, (g, st, 0, SPLIT))
        return remote(ref, ref, y_sem.at[g, st], beside)

    def round_copy(leg, u):
        unit = round_units[u]
        src, dst, where = ((s0, s2, beside), (s2, s1, below), (s1, s2, beside))[leg]
        return remote(part(src, unit), part(dst, unit), round_sem.at[leg, u], where)

    def round_got(leg, u):
        ref = part((s2, s1, s2)[leg], round_units[u])
        return remote(ref, ref, round_sem.at[leg, u], above if leg == 1 else beside)

    kept = (order[1], 0, 0, SPLIT)
    after_first = pl.ds(LANES, r2s.shape[1] - LANES)

    def ahead_copy():
        return remote(part(s0, (0, 0, 0, SPLIT)), part(s2, kept), ahead_sem.at[0], below)

    def ahead_got():
        return remote(part(s2, kept), part(s2, kept), ahead_sem.at[0], above)

    def ahead_across(mine):
        ref = part(s2, kept, c if mine else 1 - c)
        return remote(ref, ref, ahead_sem.at[1], core)

    transit = jnp.logical_and(odd, has_down)

    def send_stripe(g, st):
        @pl.when(jnp.logical_and(even, has_down))
        def _():
            for u, unit in enumerate(down_units):
                if unit[:2] == (g, st):
                    down_copy(u).start()
            for u, unit in enumerate(round_units):
                if unit[:2] == (g, st):
                    round_copy(0, u).start()

        @pl.when(odd)
        def _():
            y_copy(g, st).start()

        if (g, st) == stripes[0]:

            @pl.when(transit)
            def _():
                ahead_copy().start()

    def pass_down(u):
        round_got(0, u).wait_recv()
        round_copy(1, u).start()

    def up_copy(k):
        rows = pl.ds(k * TURNED, TURNED)
        return remote(tu.at[rows, :], tm.at[rows, :], up_sem.at[k], above)

    def up_got(k):
        ref = tm.at[pl.ds(k * TURNED, TURNED), :]
        return remote(ref, ref, up_sem.at[k], below)

    def finish(g):
        for st in range(2):
            score(g, st)
            send_stripe(g, st)
        samples_copy(g, c).start()

    def complete(i):
        g = order[i]
        samples_copy(g, 1 - c).wait_recv()

        @pl.when(has_up)
        def _():
            for q in range(4):
                rows = slice(q * (full // 4), (q + 1) * (full // 4))
                tu[i * LANES : (i + 1) * LANES, rows] = s0[g, c, rows, :].T
            for k in range(i * (LANES // TURNED), (i + 1) * (LANES // TURNED)):
                up_copy(k).start()

    def turn_own():
        def one(r, carry):
            for st in range(2):
                for q in range(4):
                    rows = slice(q * (full // 4), (q + 1) * (full // 4))
                    at = pl.multiple_of(r * WIDTH + st * LANES, LANES)
                    t0[pl.ds(at, LANES), rows] = s0[c * (groups // 2) + r, st, rows, :].T
            return carry

        lax.fori_loop(0, groups // 2, one, 0)

    def pass_some(units):
        @pl.when(transit)
        def _():
            for u in units:
                if u < len(round_units):
                    pass_down(u)

    sums(order[0])
    pl.semaphore_wait(barrier, 2 + 2 * (has_up.astype(jnp.int32) + has_down.astype(jnp.int32)))
    stat_copy(order[0]).start()
    sums(order[1])
    stat_copy(order[1]).start()
    for i, g in enumerate(order):
        stat_copy(g).wait()
        finish(g)
        if i > 0:
            complete(i - 1)
            pass_some(((), (), (0, 1), (2, 3))[i])
        if i > 0 and i + 1 < groups:
            sums(order[i + 1])
            stat_copy(order[i + 1]).start()
    complete(groups - 1)
    pass_some((4, 5))
    turn_own()

    def right(s, g):
        return jnp.concatenate([s[g, 0], s[g, 1]], axis=1)

    def column(g):
        start = g * WIDTH
        return pl.ds(start if isinstance(g, int) else pl.multiple_of(start, WIDTH), WIDTH)

    def product(left, s, g):
        acc = jnp.dot(left, right(s, g), preferred_element_type=jnp.float32)
        return (acc * (1.0 / total)).astype(jnp.bfloat16)

    def tile(k, s, g):
        obuf[k, :, column(g)] = product(t0[...], s, g)

    def tile_range(k, s, lo, hi):
        def one(g, carry):
            tile(k, s, g)
            return carry

        lax.fori_loop(lo, hi, one, 0)

    def ahead_store():
        cols = pl.ds(0, LANES)
        return pltpu.make_async_copy(obuf.at[2, :, cols], out_ref.at[2, :, cols], out_sem.at[2])

    def store(k):
        return pltpu.make_async_copy(obuf.at[k], out_ref.at[k], out_sem.at[k])

    def x1_copy(g, st, mine):
        ref = part(s1, (g, st, 0, SPLIT), c if mine else 1 - c)
        return remote(ref, ref, x1_sem.at[g, st], core)

    def x2_copy(u, mine):
        ref = part(s2, (down_units + round_units)[u], c if mine else 1 - c)
        return remote(ref, ref, x2_sem.at[u], core)

    def behind_to(start, size, k, cols):
        i = start // LANES
        at = (i // 2) * WIDTH + c * LANES + lax.rem(start, LANES)
        rows = pl.ds(pl.multiple_of(at, TURNED), size)
        return out_ref.at[k, rows, cols], {"var": b - 2, "samp": lax.rem(i, 2)}

    def r3_stripe(k, g, st):
        start = pl.multiple_of(k * TURNED, TURNED)
        rows = pl.ds(start, TURNED)
        cols = pl.ds(st * LANES, LANES)
        acc = jnp.dot(tm[rows, :], s1[g, st], preferred_element_type=jnp.float32)
        r3s[g, rows, cols] = (acc * (1.0 / total)).astype(jnp.bfloat16)
        dst, where = behind_to(start, TURNED, WIN - 1, pl.ds(g * WIDTH + st * LANES, LANES))
        remote(r3s.at[g, rows, cols], dst, r3_sem, where).start()

    def r3_group(k, g):
        start = pl.multiple_of(k * TURNED, TURNED)
        rows = pl.ds(start, TURNED)
        r3s[g, rows, :] = product(tm[rows, :], s1, g)
        dst, where = behind_to(start, TURNED, WIN - 1, column(g))
        remote(r3s.at[g, rows, :], dst, r3_sem, where).start()

    def r3_row(k, count):
        for j in range(count // 2):
            r3_group(jnp.int32(k), order[j])
        if count % 2:
            r3_stripe(jnp.int32(k), *stripes[count - 1])

    def r2_odd(k):
        rows = pl.ds(k * TURNED, TURNED)
        start = jnp.int32(k * TURNED)

        def one(g, carry):
            r2s[rows, column(g)] = product(tm[rows, :], s0, g)
            dst, where = behind_to(start, TURNED, WIN - 2, column(g))
            remote(r2s.at[rows, column(g)], dst, r2_sem, where).start()
            return carry

        lax.fori_loop(1, groups, one, 0)
        cols = pl.ds(LANES, LANES)
        acc = jnp.dot(tm[rows, :], s0[0, 1], preferred_element_type=jnp.float32)
        r2s[rows, cols] = (acc * (1.0 / total)).astype(jnp.bfloat16)
        dst, where = behind_to(start, TURNED, WIN - 2, cols)
        remote(r2s.at[rows, cols], dst, r2_sem, where).start()

    def over(lo, hi, body):
        def one(r, carry):
            body(r)
            return carry

        lax.fori_loop(lo, hi, one, 0)

    def drain_common():
        for g in range(groups):
            samples_copy(g, c).wait_send()

        @pl.when(has_up)
        def _():
            for k in range(rows_out // TURNED):
                up_copy(k).wait_send()

        @pl.when(jnp.logical_or(even, has_up))
        def _():
            for g, st in stripes:
                x1_copy(g, st, True).wait_send()

    def sent_results(buffer, sem):
        remote(buffer, buffer, sem, below).wait_send()

    def got_results(k, sem):
        ref = out_ref.at[k, :, after_first] if k == WIN - 2 else out_ref.at[k]
        remote(ref, ref, sem, above).wait_recv()

    @pl.when(even)
    def _():
        def relay(u):
            @pl.when(has_up)
            def _():
                down_got(u).wait_recv()
                relay_copy(u).start()
                x2_copy(u, True).start()

        def second(i):
            @pl.when(has_up)
            def _():
                for u, unit in enumerate(down_units):
                    if unit[0] == order[i]:
                        x2_copy(u, False).wait_recv()
                tile(2, s2, order[i])

        relay(0)
        tile_range(0, s0, 0, groups)
        store(0).start()
        for j, (g, st) in enumerate(stripes):
            y_got(g, st).wait_recv()
            x1_copy(g, st, True).start()
            if j + 1 < len(down_units):
                relay(j + 1)
            x1_copy(g, st, False).wait_recv()

            @pl.when(has_down)
            def _():
                over(0, j, lambda k: r3_stripe(k, g, st))
                up_got(j).wait_recv()
                r3_row(j, j + 1)

            if st == 1:
                tile(1, s1, g)
                if g != order[0]:
                    second(order.index(g))
        store(1).start()
        drain_common()

        @pl.when(has_down)
        def _():
            for v in range(len(down_units)):
                down_copy(v).wait_send()
            for v in range(len(round_units)):
                round_copy(0, v).wait_send()

        @pl.when(has_up)
        def _():
            for v in range(len(down_units)):
                relay_copy(v).wait_send()
                x2_copy(v, True).wait_send()
            for v, unit in enumerate(down_units):
                if unit[0] == 0:
                    x2_copy(v, False).wait_recv()
            for v in range(len(round_units)):
                round_got(2, v).wait_recv()
                x2_copy(len(down_units) + v, True).start()
            for v in range(len(round_units)):
                x2_copy(len(down_units) + v, False).wait_recv()
            tile(2, s2, 0)
            store(2).start()
            for v in range(len(round_units)):
                x2_copy(len(down_units) + v, True).wait_send()

        @pl.when(has_down)
        def _():
            sent_results(r3s, r3_sem)

        @pl.when(has_up)
        def _():
            got_results(WIN - 1, r3_sem)
            store(2).wait()

    @pl.when(odd)
    def _():
        def turn(k, count):
            @pl.when(has_down)
            def _():
                up_got(k).wait_recv()
                r2_odd(k)

            @pl.when(jnp.logical_and(has_down, has_up))
            def _():
                r3_row(k, count)

        def arrive(j):
            g, st = stripes[j]

            @pl.when(has_up)
            def _():
                for v, unit in enumerate(round_units):
                    if unit[:2] == (g, st):
                        round_got(1, v).wait_recv()
                        round_copy(2, v).start()
                for v, unit in enumerate(down_units):
                    if unit[:2] == (g, st):
                        relay_got(v).wait_recv()
                x1_copy(g, st, True).start()

        def column_of(j, rows):
            g, st = stripes[j]

            @pl.when(has_up)
            def _():
                x1_copy(g, st, False).wait_recv()

            @pl.when(jnp.logical_and(has_down, has_up))
            def _():
                over(0, rows, lambda k: r3_stripe(k, g, st))

        def first(i):
            @pl.when(has_up)
            def _():
                tile(1, s1, order[i])

        turn(0, 0)

        @pl.when(has_down)
        def _():
            for u in range(2 * groups - 2, len(round_units)):
                pass_down(u)

        tile_range(0, s0, 0, groups)
        store(0).start()

        @pl.when(has_up)
        def _():
            ahead_got().wait_recv()
            ahead_across(True).start()

        arrive(0)
        turn(1, 0)
        arrive(1)
        column_of(0, 2)
        column_of(1, 2)
        for k in range(2, len(stripes)):
            arrive(k)
            turn(k, k)
            column_of(k, k + 1)
            if k % 2 == 0:
                first(k // 2 - 1)
            if k == 3:

                @pl.when(has_up)
                def _():
                    ahead_across(False).wait_recv()
                    acc = jnp.dot(t0[...], s2[kept[0], 0], preferred_element_type=jnp.float32)
                    obuf[2, :, 0:LANES] = (acc * (1.0 / total)).astype(jnp.bfloat16)
                    ahead_store().start()

        first(groups - 1)
        store(1).start()
        drain_common()
        for g in range(groups):
            for h in range(2):
                y_copy(g, h).wait_send()

        @pl.when(has_down)
        def _():
            for v in range(len(round_units)):
                round_copy(1, v).wait_send()

        @pl.when(has_up)
        def _():
            for v in range(len(round_units)):
                round_copy(2, v).wait_send()

        @pl.when(has_down)
        def _():
            sent_results(r2s.at[:, after_first], r2_sem)
            ahead_copy().wait_send()

        @pl.when(jnp.logical_and(has_down, has_up))
        def _():
            sent_results(r3s, r3_sem)

        @pl.when(has_up)
        def _():
            got_results(WIN - 2, r2_sem)
            ahead_across(True).wait_send()
            ahead_store().wait()

        @pl.when(b + 4 < n)
        def _():
            got_results(WIN - 1, r3_sem)

    store(0).wait()
    store(1).wait()


def per_device(dosage, observed, counts):
    local, variants = dosage.shape
    n = lax.axis_size("var")
    full = local * lax.axis_size("samp")
    half = variants // 2
    groups = variants // WIDTH
    downs = len(STRAIGHT) + 2 * (groups - 1)
    rounds = len(ROUND)
    dma = pltpu.SemaphoreType.DMA
    block = pltpu.VMEM((groups, 2, full, LANES), jnp.bfloat16)
    tiles = pl.pallas_call(
        functools.partial(kernel, n, float(full)),
        out_shape=jax.ShapeDtypeStruct((WIN, half, variants), jnp.bfloat16),
        in_specs=[pl.BlockSpec(memory_space=pltpu.HBM)] * 2,
        out_specs=pl.BlockSpec(memory_space=pl.ANY),
        scratch_shapes=[
            pltpu.VMEM((groups, local, WIDTH), dosage.dtype),
            pltpu.VMEM((groups, local, WIDTH), observed.dtype),
            block,
            block,
            block,
            pltpu.VMEM((half, full), jnp.bfloat16),
            pltpu.VMEM((half, full), jnp.bfloat16),
            pltpu.VMEM((half, full), jnp.bfloat16),
            pltpu.VMEM((half, variants), jnp.bfloat16),
            pltpu.VMEM((groups, half, WIDTH), jnp.bfloat16),
            pltpu.VMEM((groups, 8, WIDTH), jnp.float32),
            pltpu.VMEM((groups, 8, WIDTH), jnp.float32),
            pltpu.VMEM((WIN - 1, half, variants), jnp.bfloat16),
            dma((groups, 2)),
            dma((groups, 2)),
            dma((groups, 2)),
            dma((downs, 2)),
            dma((downs, 2)),
            dma((groups, 2, 2)),
            dma((half // TURNED, 2)),
            dma((3, max(rounds, 1), 2)),
            dma((groups, 2, 2)),
            dma((downs + rounds, 2)),
            dma((2,)),
            dma((2,)),
            dma((2, 2)),
            dma((WIN - 1,)),
        ],
        compiler_params=pltpu.CompilerParams(
            collective_id=0, has_side_effects=True, vmem_limit_bytes=VMEM_LIMIT
        ),
    )(
        pltpu.with_memory_space_constraint(dosage, pltpu.HBM),
        pltpu.with_memory_space_constraint(observed, pltpu.HBM),
    )
    keep = jnp.arange(WIN, dtype=jnp.int32)[:, None, None] < counts[0]
    return jnp.where(keep, tiles, jnp.zeros_like(tiles))[None]


def solution(mesh):
    in_specs = (P("samp", ("region", "var")), P("samp", ("region", "var")), P(("region", "var")))
    out_specs = P(("region", "var"), None, "samp", None)
    return jax.shard_map(
        per_device, mesh=mesh, in_specs=in_specs, out_specs=out_specs, check_vma=False
    )
```
